512 devices in a mesh: row: 16 (over z_hi, y), col: 32 (over x, z_lo, core).
Axes of the slice: x: 4, y: 8, z: 8 (z_hi: 2, z_lo: 4; z = z_hi * 4 + z_lo), core: 2. Of those that a mesh axis runs over, the one named last changes fastest.
Arguments:
- psi: bfloat16 [131072, 8192], P(('row', 'col')), may hold values from -0.0625 to 0.0625
- hpsi: bfloat16 [131072, 128], P(('row', 'col')), may hold values from -0.796875 to 0.796875
- slab_counts: int32 [512], P(('row', 'col')), may hold values from 1 to 256, 98304 in all
- matrix: float32 [16, 512, 32, 256], P('row', None, 'col'), as said below
Outputs:
- reduced: float32 [16, 512, 32, 256], P('row', None, 'col')
The draws below stay inside these ranges and needn't reach their ends.
Inputs may be any that keep to these rules, and one draw needn't show every extreme that they name: Slab k's live plane waves are its first slab_counts[k] slots; the rest are padding; the counts sum to 3 * 256 * 512 // 4. The stored matrix is symmetric.
All inputs are finite; a program needn't handle non-finite values.
Results may differ from the reference program's by a relative error of at most 0.0003.
Values sent between devices are 32-bit elements; how exact they have to be, the bound alone decides.
A program may use at most 64 MiB of HBM per device.

```python
import math
import jax
import jax.numpy as jnp
import numpy as np
from jax import lax

NB = 8192
PANEL = 128
TILE = 16
G_DEV = 256
NG = 131072
N_ROW = 16
N_COL = 32
DEVICES = 512


def draw_matrix(key, part):
    first = jax.random.normal(jax.random.fold_in(key, 11), (NB, NB), jnp.float32)
    sym = (first + first.T) * 0.7071
    tiles_r = NB // (TILE * N_ROW)
    tiles_c = NB // (TILE * N_COL)
    grid = sym.reshape(tiles_r, N_ROW, TILE, tiles_c, N_COL, TILE)
    return grid.transpose(1, 0, 2, 4, 3, 5).reshape(N_ROW, NB // N_ROW, N_COL, NB // N_COL)


def raised(drawn, key, source, target, shards_of, factor):
    def block_of(axis_at):
        return (jnp.arange(drawn.shape[axis_at]) // (drawn.shape[axis_at] // shards_of)).reshape((-1,) + (1,) * (drawn.ndim - 1 - axis_at))

    near = jax.random.permutation(key, shards_of)[block_of(target)]
    second = (block_of(target) + shards_of // 2) % shards_of
    return jnp.where((block_of(source) == near) | (block_of(source) == second), factor * drawn, drawn)


def shard_levels(stream_key, shape, split, low, high):
    loudness = 1.0
    for position, parts in split:
        heights = jax.random.uniform(jax.random.fold_in(jax.random.fold_in(stream_key, 6), position), (parts,), jnp.float32, low / len(split), high / len(split))
        loudness = loudness * jnp.repeat(jnp.exp(heights), shape[position] // parts).reshape((-1,) + (1,) * (len(shape) - 1 - position))
    return loudness


def profile(amount, total, limit, slope):
    weights = [(1 << 20) // math.isqrt(grade ** slope) + 1 for grade in range(2, amount + 1)]
    surplus, given = total - limit - (amount - 1), [1] * (amount - 1)
    while surplus > 0:
        candidates = [i for i in range(amount - 1) if given[i] < limit]
        whole, left = sum([weights[i] for i in candidates]), surplus
        for i in candidates:
            more = min(limit - given[i], max(1, left * weights[i] // whole), surplus)
            given[i] = given[i] + more
            surplus = surplus - more
    return np.array([limit] + given)


def uneven_parts(own_key, number_of, total, limit, slope):
    if number_of == 2:
        one = jax.random.randint(own_key, (), max(1, total - limit), min(limit, total - 1) + 1)
        return jnp.stack([one, total - one])
    lengths = jnp.asarray(profile(number_of, total, limit, slope), jnp.int32)
    couples = (number_of - 1) // 2
    source_of, sink = lengths[1:1 + 2 * couples:2], lengths[2:2 + 2 * couples:2]
    margin = jnp.minimum(source_of - 1, limit - sink)
    passed = jax.random.randint(jax.random.fold_in(own_key, 1), (couples,), 0, 1 << 20) % (margin + 1)
    lengths = lengths.at[1:1 + 2 * couples:2].set(source_of - passed).at[2:2 + 2 * couples:2].set(sink + passed)
    return lengths[jax.random.permutation(jax.random.fold_in(own_key, 2), number_of)]


def normal_values(key, dims, scale, most, shards=(), kind=jnp.bfloat16):
    entries = jax.random.normal(key, dims, jnp.float32) * scale
    if len(shards) > 0:
        entries = shard_levels(key, dims, shards, -0.22, 0.18) * entries
    return jnp.clip(entries, min=-most, max=most).astype(kind)


def heavy_noise(key, shape, spread, reach, cuts, heavy, kind=jnp.bfloat16):
    result = spread * jax.random.normal(key, shape, jnp.float32)
    if cuts:
        result = result * shard_levels(key, shape, cuts, -0.22, 0.18)
    return jnp.clip(raised(result, jax.random.fold_in(key, 3), *heavy), -reach, reach).astype(kind)


def setup_inputs(seed: int = 0) -> dict:
    keys = jax.random.split(jax.random.key(seed), 5)
    return {
        "psi": heavy_noise(keys[0], (NG, NB), NG ** -0.5, 0.0625, ((0, 512),), (0, 1, 512, 6.0)),
        "hpsi": normal_values(keys[1], (NG, PANEL), 0.1, 0.796875, ((0, 512),)),
        "slab_counts": uneven_parts(keys[2], DEVICES, 3 * G_DEV * DEVICES // 4, G_DEV, 1).astype(jnp.int32),
        "matrix": draw_matrix(jax.random.fold_in(keys[4], 71), 0),
    }


HIGH = lax.Precision.HIGHEST

def to_full(stored):
    tiles_r = NB // (TILE * N_ROW)
    tiles_c = NB // (TILE * N_COL)
    grid = stored.reshape(N_ROW, tiles_r, TILE, N_COL, tiles_c, TILE)
    return grid.transpose(1, 0, 2, 4, 3, 5).reshape(NB, NB)

def to_stored(full):
    tiles_r = NB // (TILE * N_ROW)
    tiles_c = NB // (TILE * N_COL)
    grid = full.reshape(tiles_r, N_ROW, TILE, tiles_c, N_COL, TILE)
    return grid.transpose(1, 0, 2, 4, 3, 5).reshape(N_ROW, NB // N_ROW, N_COL, NB // N_COL)

def lower_solve(factor, rhs):
    return lax.linalg.triangular_solve(factor, rhs, left_side=True, lower=True)

def invert_shifted(shifted):
    normal = jnp.dot(shifted.T, shifted, precision=HIGH)
    factor = jnp.linalg.cholesky(normal)
    first = lower_solve(factor, shifted.T)
    return lax.linalg.triangular_solve(factor, first, left_side=True, lower=True, transpose_a=True)

def reference(psi, hpsi, slab_counts, matrix):
    valid = (jnp.arange(G_DEV, dtype=jnp.int32)[None, :] < slab_counts[:, None]).reshape(-1)
    hcols = jnp.where(valid[:, None], hpsi, jnp.zeros_like(hpsi))
    columns = lax.dot_general(psi.astype(jnp.float32), hcols.astype(jnp.float32), (((0,), (0,)), ((), ())), preferred_element_type=jnp.float32)
    full = to_full(matrix)
    corner = columns[:PANEL]
    refreshed = full.at[:, :PANEL].set(columns).at[:PANEL, :].set(columns.T)
    refreshed = refreshed.at[:PANEL, :PANEL].set(0.5 * (corner + corner.T))
    index = jnp.arange(NB, dtype=jnp.int32)
    lower = jnp.where((index >= PANEL)[:, None], columns, jnp.zeros_like(columns))
    gram = jnp.dot(lower.T, lower, precision=HIGH)
    factor = jnp.linalg.cholesky(gram)
    basis = lower_solve(factor, lower.T).T
    top = basis[PANEL:2 * PANEL]
    inverse = invert_shifted(jnp.eye(PANEL, dtype=jnp.float32) - top)
    embed = (index[:, None] == PANEL + jnp.arange(PANEL, dtype=jnp.int32)[None, :]).astype(jnp.float32)
    reflect = basis - embed
    zrows = jnp.dot(refreshed, reflect, precision=HIGH)
    ucols = jnp.dot(refreshed.T, reflect, precision=HIGH)
    wmat = jnp.dot(reflect.T, zrows, precision=HIGH)
    core = jnp.dot(jnp.dot(inverse, wmat, precision=HIGH), inverse.T, precision=HIGH)
    first = jnp.dot(reflect, jnp.dot(inverse, ucols.T, precision=HIGH), precision=HIGH)
    second = jnp.dot(jnp.dot(zrows, inverse.T, precision=HIGH) - jnp.dot(reflect, core, precision=HIGH), reflect.T, precision=HIGH)
    return to_stored(refreshed - first - second)
```

```python
import jax
import jax.numpy as jnp
from jax import lax
from jax.sharding import PartitionSpec as P
from jax.experimental import pallas as pl
from jax.experimental.pallas import tpu as pltpu

MESH = pl.DeviceIdType.MESH


def position():
    p, q = lax.axis_index("row"), lax.axis_index("col")
    return p, q, p // 8, p % 8, q // 8, (q // 2) % 4, q % 2


def device(zh, y, x, zl, c):
    return (zh * 8 + y, x * 8 + zl * 2 + c)


def send(src, dst, send_sem, recv_sem, target):
    return pltpu.make_async_remote_copy(
        src_ref=src, dst_ref=dst, send_sem=send_sem, recv_sem=recv_sem,
        device_id=target, device_id_type=MESH,
    )


def panel_kernel(part, rows_out, cols_out, theirs, wa, wb, ra1, rb1, a1, b1, ra2, rb2,
                 ab2, r3, own, ss, rs, ss_r, rs_r, ss_c, rs_c):
    p, q, zh, y, x, zl, c = position()
    z = zh * 4 + zl
    first = c == 0
    f = jnp.where(first, y, z)
    s = jnp.where(first, z, y)

    def at(xx, ff, sf):
        yy, zz = jnp.where(first, ff, sf), jnp.where(first, sf, ff)
        return device(zz // 4, yy, xx, zz % 4, c)

    target_row = q % 16
    tile = 2 * p + q // 16
    partner = device(zh, y, x, zl, 1 - c)
    barrier = pltpu.get_barrier_semaphore()

    def hail(who):
        pl.semaphore_signal(barrier, inc=1, device_id=who, device_id_type=MESH)

    hail(partner)
    for d in range(1, 4):
        hail(at((x + d) % 4, f, s))
    for d in range(1, 8):
        hail(at(x, (f + d) % 8, s))
        hail(at(x, f, (s + d) % 8))

    def hail_row(d, _):
        hail(((p + d) % 16, q))
        return 0

    lax.fori_loop(1, 16, hail_row, 0)

    def hail_owner(i, _):
        who_p, who_q = i // 2, p + 16 * (i % 2)

        @pl.when((who_p != p) | (who_q != q))
        def _():
            hail((who_p, who_q))
        return 0

    lax.fori_loop(0, 32, hail_owner, 0)
    pl.semaphore_wait(barrier, 1 + 3 + 7 + 7 + 15 + 31 + jnp.where(target_row != p, 1, 0))

    swap = send(part.at[:, :, :, :, 1 - c], theirs, ss.at[0], rs.at[0], partner)
    swap.start()
    swap.wait()

    def join(i, _):
        ff, sf = i // 8, i % 8
        yy, zz = jnp.where(first, ff, sf), jnp.where(first, sf, ff)
        hh, ll = zz // 4, zz % 4
        for xx in range(4):
            total = part[hh, yy, xx, ll, c] + theirs[hh, yy, xx, ll]
            wa[xx, ff, sf] = total[:8]
            wb[ff, xx, sf] = total[8:]
        return 0

    lax.fori_loop(0, 64, join, 0)
    copies_a, copies_b = [], []
    for d in range(1, 4):
        xx = (x + d) % 4
        copies_a.append(send(wa.at[xx], ra1.at[d - 1], ss.at[d], rs.at[d], at(xx, f, s)))
        copies_a[-1].start()
    for d in range(1, 8):
        ff = (f + d) % 8
        copies_b.append(send(wb.at[ff], rb1.at[d - 1], ss.at[3 + d], rs.at[3 + d], at(x, ff, s)))
        copies_b[-1].start()
    for copy in copies_b:
        copy.wait()

    def sum_b1(i, _):
        total = wb[f, i]
        for d in range(7):
            total += rb1[d, i]
        b1[i] = total
        return 0

    lax.fori_loop(0, 4, sum_b1, 0)
    copies_b = []
    for d in range(1, 4):
        xx = (x + d) % 4
        copies_b.append(send(b1.at[xx], rb2.at[d - 1], ss.at[10 + d], rs.at[10 + d], at(xx, f, s)))
        copies_b[-1].start()
    for copy in copies_a:
        copy.wait()

    def sum_a1(i, _):
        total = wa[x, i]
        for d in range(3):
            total += ra1[d, i]
        a1[i] = total
        return 0

    lax.fori_loop(0, 8, sum_a1, 0)
    copies_a = []
    for d in range(1, 8):
        ff = (f + d) % 8
        copies_a.append(send(a1.at[ff], ra2.at[d - 1], ss.at[13 + d], rs.at[13 + d], at(x, ff, s)))
        copies_a[-1].start()
    for copy in copies_b:
        copy.wait()
    ab2[:, 1] = b1[x] + rb2[0] + rb2[1] + rb2[2]
    for copy in copies_a:
        copy.wait()
    total = a1[f]
    for d in range(7):
        total += ra2[d]
    ab2[:, 0] = total
    copies = []
    for d in range(1, 8):
        sf = (s + d) % 8
        copies.append(send(ab2.at[sf], r3.at[d - 1], ss.at[20 + d], rs.at[20 + d], at(x, f, sf)))
        copies[-1].start()
    for copy in copies:
        copy.wait()
    total = ab2[s]
    for d in range(7):
        total += r3[d]
    own[...] = total.reshape(16, 128)
    cols_out[p] = own[...]

    def to_column(d):
        return send(own, cols_out.at[p], ss_c.at[d], rs_c.at[p], ((p + d) % 16, q))

    def to_row(d):
        return send(own, rows_out.at[tile], ss_r.at[d], rs_r.at[tile], (target_row, (q + d) % 32))

    for d in range(1, 16):
        to_column(d).start()
    for d in range(1, 32):
        to_row(d).start()

    @pl.when(target_row == p)
    def _():
        rows_out[tile] = own[...]

    @pl.when(target_row != p)
    def _():
        to_row(0).start()

    for d in range(1, 16):
        to_column(d).wait_send()
    for d in range(1, 32):
        to_row(d).wait_send()

    @pl.when(target_row != p)
    def _():
        to_row(0).wait_send()

    for d in range(1, 16):
        j = (p + d) % 16
        send(own, cols_out.at[j], ss_c.at[d], rs_c.at[j], (j, q)).wait_recv()

    def from_owner(i, _):
        @pl.when((i // 2 != p) | (p + 16 * (i % 2) != q))
        def _():
            send(own, rows_out.at[i], ss_r.at[0], rs_r.at[i], (p, q)).wait_recv()
        return 0

    lax.fori_loop(0, 32, from_owner, 0)


def panel_sum(part):
    f32 = jnp.float32
    vmem = pl.BlockSpec(memory_space=pltpu.VMEM)
    dma = pltpu.SemaphoreType.DMA
    rows, cols = pl.pallas_call(
        panel_kernel,
        name="panel_sum",
        out_shape=(jax.ShapeDtypeStruct((32, 16, 128), f32), jax.ShapeDtypeStruct((16, 16, 128), f32)),
        in_specs=[vmem],
        out_specs=(vmem, vmem),
        scratch_shapes=[
            pltpu.VMEM((2, 8, 4, 4, 16, 128), f32),
            pltpu.VMEM((4, 8, 8, 8, 128), f32),
            pltpu.VMEM((8, 4, 8, 8, 128), f32),
            pltpu.VMEM((3, 8, 8, 8, 128), f32),
            pltpu.VMEM((7, 4, 8, 8, 128), f32),
            pltpu.VMEM((8, 8, 8, 128), f32),
            pltpu.VMEM((4, 8, 8, 128), f32),
            pltpu.VMEM((7, 8, 8, 128), f32),
            pltpu.VMEM((3, 8, 8, 128), f32),
            pltpu.VMEM((8, 2, 8, 128), f32),
            pltpu.VMEM((7, 2, 8, 128), f32),
            pltpu.VMEM((16, 128), f32),
            dma((28,)), dma((28,)), dma((32,)), dma((32,)), dma((16,)), dma((16,)),
        ],
        compiler_params=pltpu.CompilerParams(collective_id=1, has_side_effects=True, vmem_limit_bytes=48 << 20),
    )(part.reshape(2, 8, 4, 4, 2, 16, 128))
    return rows.reshape(512, 128), cols.reshape(256, 128)


TILE = 16


HIGH = lax.Precision.HIGHEST


def filled_up(lines, devices):
    spare = -len(lines) % devices
    return jnp.pad(lines, [(0, spare)] + [(0, 0)] * (lines.ndim - 1))


def laid_out(blocks, dim):
    blocks = jnp.moveaxis(blocks, 0, dim)
    lengths = blocks.shape
    return blocks.reshape(*lengths[:dim], lengths[dim] * lengths[dim + 1], *lengths[dim + 2 :])


def sent_to_all(array, axis):
    devices = lax.axis_size(axis)
    return lax.all_to_all(
        jnp.broadcast_to(array[None], (devices, *array.shape)), axis, 0, 0, tiled=True
    )


def gather_directly(array, axis, dim):
    return laid_out(sent_to_all(array, axis), dim)


def split_up(array, dim, devices):
    before, after = (array.shape[:dim], array.shape[dim + 1 :])
    return jnp.moveaxis(array.reshape(*before, devices, -1, *after), dim, 0)


def summed_on_arrival(array, axis, dim):
    blocks = split_up(array, dim, lax.axis_size(axis))
    arrived = lax.all_to_all(blocks, axis, split_axis=0, concat_axis=0, tiled=True)
    return arrived.sum(axis=0)


def sum_by_parts(array, axes):
    padded = filled_up(array, lax.axis_size(axes))
    whole = gather_directly(summed_on_arrival(padded, axes, 0), axes, 0)
    return lax.slice_in_dim(whole, 0, len(array)).reshape(array.shape)


def together(arrays, axis):
    flat, at, gathered = (jnp.concatenate([a.reshape(-1) for a in arrays]), 0, [])
    subtotal = sum_by_parts(flat, axis)
    for a in arrays:
        gathered.append(subtotal[at : at + a.size].reshape(a.shape))
        at += a.size
    return tuple(gathered)


def sum_by_parts_2(array, axes):
    lines = array.reshape(-1, array.shape[-1])
    padded = filled_up(lines, lax.axis_size(axes))
    whole = gather_directly(summed_on_arrival(padded, axes, 0), axes, 0)
    return lax.slice_in_dim(whole, 0, len(lines)).reshape(array.shape)


def over_copies(array, axis):
    return sent_to_all(array, axis).sum(axis=0)


def lower_solve(factor, rhs):
    return lax.linalg.triangular_solve(factor, rhs, left_side=True, lower=True)


def invert_shifted(shifted):
    normal = jnp.dot(shifted.T, shifted, precision=HIGH)
    factor = jnp.linalg.cholesky(normal)
    first = lower_solve(factor, shifted.T)
    return lax.linalg.triangular_solve(factor, first, left_side=True, lower=True, transpose_a=True)


def per_device(psi, hpsi, slab_counts, matrix):
    prow_id = lax.axis_index("row")
    pcol_id = lax.axis_index("col")
    n_row = lax.axis_size("row")
    n_col = lax.axis_size("col")
    slots = psi.shape[0]
    panel = hpsi.shape[1]
    local_rows = matrix.shape[1]
    local_cols = matrix.shape[3]
    tiles_r = local_rows // TILE
    tiles_c = local_cols // TILE
    valid = jnp.arange(slots, dtype=jnp.int32) < slab_counts[0]
    hcols = jnp.where(valid[:, None], hpsi, jnp.zeros_like(hpsi))
    local_r = jnp.arange(local_rows, dtype=jnp.int32)
    local_c = jnp.arange(local_cols, dtype=jnp.int32)
    row_global = (local_r // TILE * n_row + prow_id) * TILE + local_r % TILE
    col_global = (local_c // TILE * n_col + pcol_id) * TILE + local_c % TILE
    partial_value = lax.dot_general(
        psi, hcols, (((0,), (0,)), ((), ())), preferred_element_type=jnp.float32
    )
    prow, scols = panel_sum(partial_value)
    span = jnp.arange(panel, dtype=jnp.int32)
    lower_r = jnp.where((row_global >= panel)[:, None], prow, jnp.zeros_like(prow))
    lower_c = jnp.where((col_global >= panel)[:, None], scols, jnp.zeros_like(scols))
    top_select = (row_global[None, :] == panel + span[:, None]).astype(jnp.float32)
    gram_part = jnp.dot(lower_r.T, lower_r, precision=HIGH)
    top_part = jnp.dot(top_select, prow, precision=HIGH)
    gram, top_rows = together((gram_part, top_part), "row")
    factor = jnp.linalg.cholesky(gram)
    basis_r = lower_solve(factor, lower_r.T).T
    basis_c = lower_solve(factor, lower_c.T).T
    top = lower_solve(factor, top_rows.T).T
    inverse = invert_shifted(jnp.eye(panel, dtype=jnp.float32) - top)
    embed_r = (row_global[:, None] == panel + span[None, :]).astype(jnp.float32)
    embed_c = (col_global[:, None] == panel + span[None, :]).astype(jnp.float32)
    reflect_r = basis_r - embed_r
    reflect_c = basis_c - embed_c
    stored = matrix[0, :, 0, :]
    col_select = (col_global[None, :] == span[:, None]).astype(jnp.float32)
    row_select = (row_global[None, :] == span[:, None]).astype(jnp.float32)
    left = jnp.dot(prow, col_select, precision=HIGH)
    upper = lax.dot_general(row_select, scols, (((0,), (1,)), ((), ())), precision=HIGH)
    inside_r = (row_global < panel)[:, None]
    inside_c = (col_global < panel)[None, :]
    refreshed = jnp.where(
        inside_r & inside_c,
        0.5 * (left + upper),
        jnp.where(inside_c, left, jnp.where(inside_r, upper, stored)),
    )
    zpart = jnp.dot(refreshed, reflect_c, precision=HIGH)
    zrows = sum_by_parts_2(zpart, "col")
    upart = lax.dot_general(refreshed, reflect_r, (((0,), (0,)), ((), ())), precision=HIGH)
    ucols = sum_by_parts_2(upart, "row")
    wmat = over_copies(jnp.dot(reflect_r.T, zrows, precision=HIGH), "row")
    core = jnp.dot(jnp.dot(inverse, wmat, precision=HIGH), inverse.T, precision=HIGH)
    first = jnp.dot(reflect_r, jnp.dot(inverse, ucols.T, precision=HIGH), precision=HIGH)
    second = jnp.dot(
        jnp.dot(zrows, inverse.T, precision=HIGH) - jnp.dot(reflect_r, core, precision=HIGH),
        reflect_c.T,
        precision=HIGH,
    )
    return (refreshed - first - second)[None, :, None, :]


def solution(mesh):
    in_specs = (
        P(("row", "col"), None),
        P(("row", "col"), None),
        P(("row", "col")),
        P("row", None, "col", None),
    )
    out_specs = P("row", None, "col", None)
    return jax.shard_map(
        per_device, mesh=mesh, in_specs=in_specs, out_specs=out_specs, check_vma=False
    )
```

```python
import jax
import jax.numpy as jnp
from jax import lax
from jax.sharding import PartitionSpec as P
from jax.experimental import pallas as pl
from jax.experimental.pallas import tpu as pltpu

MESH = pl.DeviceIdType.MESH
HIGH = lax.Precision.HIGHEST
F32, BF16 = jnp.float32, jnp.bfloat16


def position():
    p, q = lax.axis_index("row"), lax.axis_index("col")
    return p, q, p // 8, p % 8, q // 8, (q // 2) % 4, q % 2


def device(zh, y, x, zl, c):
    return (zh * 8 + y, x * 8 + zl * 2 + c)


def send(src, dst, send_sem, recv_sem, target):
    return pltpu.make_async_remote_copy(
        src_ref=src, dst_ref=dst, send_sem=send_sem, recv_sem=recv_sem,
        device_id=target, device_id_type=MESH,
    )


def dot(a, b, ca, cb, precision=None):
    return lax.dot_general(
        a, b, (((ca,), (cb,)), ((), ())), precision=precision, preferred_element_type=F32
    )


def halves(a):
    high = a.astype(BF16)
    return high, (a - high.astype(F32)).astype(BF16)


def dot3(a, b, ca, cb):
    (ah, al), (bh, bl) = halves(a), halves(b)
    return dot(ah, bh, ca, cb) + (dot(ah, bl, ca, cb) + dot(al, bh, ca, cb))


def thirds(a):
    high = a.astype(BF16).astype(F32)
    rest = a - high
    middle = rest.astype(BF16).astype(F32)
    return high, middle, rest - middle


def outer(a, b):
    (ah, am, al), (bh, bm, bl) = thirds(a), thirds(b)
    left = jnp.concatenate([ah, ah, am, am, ah, al], 0).astype(BF16)
    right = jnp.concatenate([bh, bm, bh, bm, bl, bh], 0).astype(BF16)
    return dot(left, right, 0, 0)


def spread_columns(rows, base):
    turned = pltpu.roll(rows, (128 - base) % 128, 1)
    return [jnp.broadcast_to(turned[:, j : j + 1], (8, 128)) for j in range(8)]


def cholesky_block(k, a, ut):
    base = pl.multiple_of(8 * k, 8)
    sub = lax.broadcasted_iota(jnp.int32, (8, 128), 0)
    lane = lax.broadcasted_iota(jnp.int32, (8, 128), 1)
    rows = a[pl.ds(base, 8), :]
    cols = spread_columns(rows, base)
    for j in range(8):
        pivot = cols[j][j : j + 1]
        inv = lax.rsqrt(pivot)
        inv = inv * (1.5 - 0.5 * pivot * inv * inv)
        unit = rows[j : j + 1] * inv
        factor = jnp.where(sub > j, cols[j] * inv, 0.0)
        rows = jnp.where(sub == j, unit, rows - factor * unit)
        for i in range(j + 1, 8):
            cols[i] = cols[i] - factor * (cols[i][j : j + 1] * inv)
    done = jnp.where(lane >= base + sub, rows, 0.0)
    ut[pl.ds(base, 8), :] = done
    a[...] -= outer(done, done)


def inverse_block(k, n, t, lower, upper):
    base = pl.multiple_of(8 * k, 8)
    sub = lax.broadcasted_iota(jnp.int32, (8, 128), 0)
    rows, turned = n[pl.ds(base, 8), :], t[pl.ds(base, 8), :]
    rc, tc = spread_columns(rows[:, :128], base), spread_columns(turned[:, :128], base)
    scale = jnp.zeros((8, 128), F32)
    for j in range(8):
        inv = 1.0 / rc[j][j : j + 1]
        scale = jnp.where(sub == j, inv, scale)
        down = jnp.where(sub > j, rc[j] * inv, 0.0)
        across = jnp.where(sub > j, tc[j] * inv, 0.0)
        rows = rows - jnp.concatenate([down, down], 1) * rows[j : j + 1]
        turned = turned - jnp.concatenate([across, across], 1) * turned[j : j + 1]
        for i in range(j + 1, 8):
            rc[i] = rc[i] - down * rc[i][j : j + 1]
            tc[i] = tc[i] - across * tc[i][j : j + 1]
    turned = turned * jnp.concatenate([scale, scale], 1)
    lower[pl.ds(base, 8), :] = rows[:, 128:]
    upper[pl.ds(base, 8), :] = turned[:, 128:]
    n[...] -= outer(turned[:, :128], rows)
    t[...] -= outer(rows[:, :128], turned)


def step_kernel(part, stored, out, theirs, wa, wb, ra1, rb1, a1, b1, ra2, rb2, ab2, r3, own,
                srow, scol, mh, slr, slc, small, gx, gfull, s1, m1c, m1r, xpart, xin, xown,
                xr, xc, work, ut, n, t, lower, upper, zr, zc, wx, wfull, piece,
                ss, rs, ss_r, rs_r, ss_c, rs_c, ss_g, rs_g, ss_h, rs_h, ss_s, rs_s,
                ss_m, rs_m, ss_k, rs_k, ss_x, rs_x, ss_y, rs_y, ss_z, rs_z,
                ss_w, rs_w, ss_v, rs_v):
    p, q, zh, y, x, zl, c = position()
    z = zh * 4 + zl
    first = c == 0
    f = jnp.where(first, y, z)
    s = jnp.where(first, z, y)
    half, slot = q // 16, q % 16
    on_diagonal = slot == p
    piece_at = q // 2

    def at(xx, ff, sf):
        yy, zz = jnp.where(first, ff, sf), jnp.where(first, sf, ff)
        return device(zz // 4, yy, xx, zz % 4, c)

    def loop(start, stop, body):
        def step(i, carry):
            body(i)
            return carry
        lax.fori_loop(start, stop, step, 0)

    partner = device(zh, y, x, zl, 1 - c)
    barrier = pltpu.get_barrier_semaphore()

    def hail(who):
        pl.semaphore_signal(barrier, inc=1, device_id=who, device_id_type=MESH)

    def hail_unless_me(who):
        @pl.when((who[0] != p) | (who[1] != q))
        def _():
            hail(who)

    hail(partner)
    for d in range(1, 4):
        hail(at((x + d) % 4, f, s))
    for d in range(1, 8):
        hail(at(x, (f + d) % 8, s))
        hail(at(x, f, (s + d) % 8))
    loop(1, 16, lambda d: hail(((p + d) % 16, q)))
    loop(1, 32, lambda d: hail((p, (q + d) % 32)))
    loop(0, 32, lambda i: hail_unless_me((i % 16, p + 16 * (i // 16))))
    loop(0, 16, lambda j: hail_unless_me((slot, 16 * half + j)))
    pl.semaphore_wait(barrier, 18 + 15 + 31 + 31 + 15 + 2 * jnp.where(on_diagonal, 0, 1))

    swap = send(part.at[:, :, :, :, 1 - c], theirs, ss.at[0], rs.at[0], partner)
    swap.start()
    swap.wait()

    def join(i, _):
        ff, sf = i // 8, i % 8
        yy, zz = jnp.where(first, ff, sf), jnp.where(first, sf, ff)
        hh, ll = zz // 4, zz % 4
        for xx in range(4):
            total = part[hh, yy, xx, ll, c] + theirs[hh, yy, xx, ll]
            wa[xx, ff, sf] = total[:8]
            wb[ff, xx, sf] = total[8:]
        return 0

    lax.fori_loop(0, 64, join, 0)
    copies_a, copies_b = [], []
    for d in range(1, 4):
        xx = (x + d) % 4
        copies_a.append(send(wa.at[xx], ra1.at[d - 1], ss.at[d], rs.at[d], at(xx, f, s)))
        copies_a[-1].start()
    for d in range(1, 8):
        ff = (f + d) % 8
        copies_b.append(send(wb.at[ff], rb1.at[d - 1], ss.at[3 + d], rs.at[3 + d], at(x, ff, s)))
        copies_b[-1].start()
    for copy in copies_b:
        copy.wait()

    def sum_b1(i, _):
        total = wb[f, i]
        for d in range(7):
            total += rb1[d, i]
        b1[i] = total
        return 0

    lax.fori_loop(0, 4, sum_b1, 0)
    copies_b = []
    for d in range(1, 4):
        xx = (x + d) % 4
        copies_b.append(send(b1.at[xx], rb2.at[d - 1], ss.at[10 + d], rs.at[10 + d], at(xx, f, s)))
        copies_b[-1].start()
    for copy in copies_a:
        copy.wait()

    def sum_a1(i, _):
        total = wa[x, i]
        for d in range(3):
            total += ra1[d, i]
        a1[i] = total
        return 0

    lax.fori_loop(0, 8, sum_a1, 0)
    copies_a = []
    for d in range(1, 8):
        ff = (f + d) % 8
        copies_a.append(send(a1.at[ff], ra2.at[d - 1], ss.at[13 + d], rs.at[13 + d], at(x, ff, s)))
        copies_a[-1].start()
    for copy in copies_b:
        copy.wait()
    ab2[:, 1] = b1[x] + rb2[0] + rb2[1] + rb2[2]
    for copy in copies_a:
        copy.wait()
    total = a1[f]
    for d in range(7):
        total += ra2[d]
    ab2[:, 0] = total
    copies = []
    for d in range(1, 8):
        sf = (s + d) % 8
        copies.append(send(ab2.at[sf], r3.at[d - 1], ss.at[20 + d], rs.at[20 + d], at(x, f, sf)))
        copies[-1].start()
    for copy in copies:
        copy.wait()
    total = ab2[s]
    for d in range(7):
        total += r3[d]
    own[...] = total.reshape(16, 128)
    scol[p] = own[...]

    def to_row_group(src, dst, sem, landed):
        return lambda d: send(src, dst, sem.at[d], landed, ((p + d) % 16, q))

    def to_col_group(src, dst, sem, landed):
        return lambda d: send(src, dst, sem.at[d], landed, (p, (q + d) % 32))

    def start_all(copy, stop):
        loop(1, stop, lambda d: copy(d).start())

    def sent_all(copy, stop):
        loop(1, stop, lambda d: copy(d).wait_send())

    def landed(dst, sem):
        send(dst, dst, ss.at[0], sem, (p, q)).wait_recv()

    put_c = to_row_group(own, scol.at[p], ss_c, rs_c.at[p])
    row_slot = 16 * half + p

    def put_r(d):
        return send(own, srow.at[row_slot], ss_r.at[d], rs_r.at[row_slot], (slot, (q + d) % 32))

    start_all(put_c, 16)
    start_all(put_r, 32)

    @pl.when(on_diagonal)
    def _():
        srow[row_slot] = own[...]

    @pl.when(jnp.logical_not(on_diagonal))
    def _():
        put_r(0).start()

    loop(1, 16, lambda d: landed(scol.at[(p + d) % 16], rs_c.at[(p + d) % 16]))

    def take_row(i):
        @pl.when((i % 16 != p) | (p + 16 * (i // 16) != q))
        def _():
            landed(srow.at[i], rs_r.at[i])

    loop(0, 32, take_row)

    lane = lax.broadcasted_iota(jnp.int32, (16, 128), 1)
    in_left = (lane < 16) & (q < 8)
    zero = jnp.zeros((16, 128), F32)

    def refresh(i):
        tile = srow[i]
        slr[i] = jnp.where((i == 0) & (p < 8), zero, tile)
        left = pltpu.roll(tile, (128 - 16 * (q % 8)) % 128, 1)
        old = stored[2 * (i % 16) + i // 16]
        mh[i, :, :128] = jnp.where(in_left, left, old[:, :128])
        mh[i, :, 128:] = old[:, 128:]

    loop(0, 32, refresh)
    slc[...] = scol[...]

    @pl.when(q < 8)
    def _():
        slc[0] = zero

    @pl.when(p < 8)
    def _():
        turned = pltpu.roll(scol[...].reshape(256, 128), (128 - 16 * (p % 8)) % 128, 1)
        upper_rows = turned.T[:16]
        mh[0, :, :128] = jnp.where(
            in_left, 0.5 * (mh[0, :, :128] + upper_rows[:, :128]), upper_rows[:, :128]
        )
        mh[0, :, 128:] = upper_rows[:, 128:]

    low = slr[...].reshape(512, 128)
    small[...] = dot(low, low, 0, 0, HIGH)
    gx[p] = small[pl.ds(pl.multiple_of(8 * piece_at, 8), 8), :]
    put_g = to_row_group(gx.at[p], gx.at[p], ss_g, rs_g.at[p])
    start_all(put_g, 16)
    from_panel = jnp.maximum(p - 8, 0)
    put_s = to_row_group(srow.at[0], s1.at[from_panel], ss_s, rs_s.at[from_panel])

    @pl.when(p >= 8)
    def _():
        s1[from_panel] = srow[0]
        start_all(put_s, 16)

    xpart[...] = dot3(mh[...].reshape(512, 256), slc[...].reshape(256, 128), 1, 0).reshape(32, 16, 128)

    def put_x(d):
        to = (q + d) % 32
        return send(xpart.at[to], xin.at[q], ss_x.at[d], rs_x.at[q], (p, to))

    start_all(put_x, 32)
    put_m = to_row_group(mh.at[0], m1c.at[from_panel], ss_m, rs_m.at[from_panel])
    rim = 8 * half + from_panel

    def put_k(d):
        return send(mh.at[0], m1r.at[rim], ss_k.at[d], rs_k.at[rim], (slot, (q + d) % 32))

    @pl.when(p >= 8)
    def _():
        m1c[from_panel] = mh[0]

    @pl.when((p >= 8) & on_diagonal)
    def _():
        m1r[rim] = mh[0]

    def all_landed(buffer, sem, count, me):
        loop(1, count, lambda d: landed(buffer.at[(me + d) % count], sem.at[(me + d) % count]))

    def total_of(buffer, count):
        total = buffer[0]
        for i in range(1, count):
            total += buffer[i]
        return total

    def put_piece(full, sem, got):
        def copy(d):
            to = (piece_at + d) % 16
            return send(full.at[piece_at], full.at[piece_at], sem.at[d], got.at[piece_at], (p, 2 * to + c))
        return copy

    all_landed(gx, rs_g, 16, p)
    gfull[piece_at] = total_of(gx, 16)
    put_h = put_piece(gfull, ss_h, rs_h)
    start_all(put_h, 16)

    all_landed(xin, rs_x, 32, q)
    xin[q] = xpart[q]
    xown[...] = total_of(xin, 32)
    xr[q] = xown[...]
    put_y = to_col_group(xown, xr.at[q], ss_y, rs_y.at[q])
    start_all(put_y, 32)

    def put_z(d):
        return send(xown, xc.at[slot], ss_z.at[d], rs_z.at[slot], ((p + d) % 16, p + 16 * half))

    start_all(put_z, 16)

    @pl.when(on_diagonal)
    def _():
        xc[slot] = xown[...]

    @pl.when(jnp.logical_not(on_diagonal))
    def _():
        put_z(0).start()

    @pl.when(p >= 8)
    def _():
        start_all(put_k, 32)
        start_all(put_m, 16)

    @pl.when((p >= 8) & jnp.logical_not(on_diagonal))
    def _():
        put_k(0).start()

    all_landed(gfull, rs_h, 16, piece_at)
    gram = gfull[...].reshape(128, 128)
    work[...] = gram
    loop(0, 16, lambda k: cholesky_block(k, work, ut))

    def take_from_panel(i):
        @pl.when(i + 8 != p)
        def _():
            landed(s1.at[i], rs_s.at[i])
            landed(m1c.at[i], rs_m.at[i])

    loop(0, 8, take_from_panel)
    tops = s1[...].reshape(128, 128)
    normal = gram - dot(ut[...], tops, 0, 0, HIGH)
    eye = (
        lax.broadcasted_iota(jnp.int32, (128, 128), 0) == lax.broadcasted_iota(jnp.int32, (128, 128), 1)
    ).astype(F32)
    n[:, :128] = normal
    n[:, 128:] = eye
    t[:, :128] = normal.T
    t[:, 128:] = eye

    @pl.when(p >= 8)
    def _():
        slr[0] -= ut[pl.ds(pl.multiple_of(16 * from_panel, 16), 16), :]

    @pl.when((q >= 8) & (q < 16))
    def _():
        slc[0] -= ut[pl.ds(pl.multiple_of(16 * jnp.clip(q - 8, 0, 7), 16), 16), :]

    all_landed(xr, rs_y, 32, q)

    def take_xc(j):
        @pl.when((slot != p) | (16 * half + j != q))
        def _():
            landed(xc.at[j], rs_z.at[j])

    loop(0, 16, take_xc)

    def take_rim(i):
        @pl.when((i % 8 + 8 != p) | (p + 16 * (i // 8) != q))
        def _():
            landed(m1r.at[i], rs_k.at[i])

    loop(0, 16, take_rim)
    root = ut[...]
    for h in range(2):
        zr[pl.ds(256 * h, 256), :] = xr[pl.ds(16 * h, 16)].reshape(256, 128) - dot3(
            m1r[pl.ds(8 * h, 8)].reshape(128, 256), root, 0, 0
        )
    zc[...] = xc[...].reshape(256, 128) - dot3(m1c[...].reshape(128, 256), root, 0, 0)
    small[...] = dot3(slr[...].reshape(512, 128), zr[...], 0, 0)
    wx[p] = small[pl.ds(pl.multiple_of(8 * piece_at, 8), 8), :]
    put_w = to_row_group(wx.at[p], wx.at[p], ss_w, rs_w.at[p])
    start_all(put_w, 16)
    loop(0, 10, lambda k: inverse_block(k, n, t, lower, upper))
    all_landed(wx, rs_w, 16, p)
    wfull[piece_at] = total_of(wx, 16)
    put_v = put_piece(wfull, ss_v, rs_v)
    start_all(put_v, 16)
    loop(10, 16, lambda k: inverse_block(k, n, t, lower, upper))
    inverse_t = dot(lower[...], upper[...], 0, 0, HIGH)
    small[...] = inverse_t
    acols = dot3(zc[...], inverse_t, 1, 0)
    all_landed(wfull, rs_v, 16, piece_at)
    core = dot(
        dot(small[...], wfull[...].reshape(128, 128), 0, 0, HIGH), small[...], 1, 0, HIGH
    )
    right = jnp.concatenate([acols, slc[...].reshape(256, 128)], 1)
    rh, rl = halves(right)
    for h in range(4):
        rows = slr[pl.ds(8 * h, 8)].reshape(128, 128)
        brows = dot3(zr[pl.ds(128 * h, 128), :], small[...], 1, 0) - dot3(rows, core, 1, 0)
        lh, ll = halves(jnp.concatenate([rows, brows], 1))
        change = dot(lh, rh, 1, 1) + (dot(lh, rl, 1, 1) + dot(ll, rh, 1, 1))
        for i in range(8):
            at_tile = 8 * h + i
            out[2 * (at_tile % 16) + at_tile // 16] = mh[at_tile] - change[16 * i : 16 * i + 16]

    sent_all(put_c, 16)
    sent_all(put_r, 32)
    sent_all(put_g, 16)
    sent_all(put_h, 16)
    sent_all(put_x, 32)
    sent_all(put_y, 32)
    sent_all(put_z, 16)
    sent_all(put_w, 16)
    sent_all(put_v, 16)

    @pl.when(jnp.logical_not(on_diagonal))
    def _():
        put_r(0).wait_send()
        put_z(0).wait_send()

    @pl.when(p >= 8)
    def _():
        sent_all(put_s, 16)
        sent_all(put_m, 16)
        sent_all(put_k, 32)

    @pl.when((p >= 8) & jnp.logical_not(on_diagonal))
    def _():
        put_k(0).wait_send()


def step(part, stored):
    vmem = pl.BlockSpec(memory_space=pltpu.VMEM)

    def room(*dims):
        return pltpu.VMEM(dims, F32)

    sems = [28, 28, 32, 32, 16, 16, 16, 16, 16, 16, 16, 8, 16, 8, 32, 16, 32, 32, 32, 32, 16, 16, 16, 16, 16, 16]
    return pl.pallas_call(
        step_kernel,
        name="step",
        out_shape=jax.ShapeDtypeStruct((32, 16, 256), F32),
        in_specs=[vmem, vmem],
        out_specs=vmem,
        scratch_shapes=[
            room(2, 8, 4, 4, 16, 128), room(4, 8, 8, 8, 128), room(8, 4, 8, 8, 128),
            room(3, 8, 8, 8, 128), room(7, 4, 8, 8, 128), room(8, 8, 8, 128), room(4, 8, 8, 128),
            room(7, 8, 8, 128), room(3, 8, 8, 128), room(8, 2, 8, 128), room(7, 2, 8, 128),
            room(16, 128),
            room(32, 16, 128), room(16, 16, 128), room(32, 16, 256), room(32, 16, 128),
            room(16, 16, 128), room(128, 128), room(16, 8, 128), room(16, 8, 128),
            room(8, 16, 128), room(8, 16, 256), room(16, 16, 256), room(32, 16, 128),
            room(32, 16, 128), room(16, 128), room(32, 16, 128), room(16, 16, 128),
            room(128, 128), room(128, 128), room(128, 256), room(128, 256), room(128, 128),
            room(128, 128), room(512, 128), room(256, 128), room(16, 8, 128), room(16, 8, 128),
            room(8, 128),
        ] + [pltpu.SemaphoreType.DMA((k,)) for k in sems],
        compiler_params=pltpu.CompilerParams(
            collective_id=1, has_side_effects=True, vmem_limit_bytes=56 << 20
        ),
    )(part.reshape(2, 8, 4, 4, 2, 16, 128), stored)


def per_device(psi, hpsi, slab_counts, matrix):
    slots = psi.shape[0]
    valid = jnp.arange(slots, dtype=jnp.int32) < slab_counts[0]
    hcols = jnp.where(valid[:, None], hpsi, jnp.zeros_like(hpsi))
    part = dot(psi, hcols, 0, 0)
    return step(part, matrix.reshape(32, 16, 256)).reshape(matrix.shape)


def solution(mesh):
    in_specs = (
        P(("row", "col"), None),
        P(("row", "col"), None),
        P(("row", "col")),
        P("row", None, "col", None),
    )
    out_specs = P("row", None, "col", None)
    return jax.shard_map(
        per_device, mesh=mesh, in_specs=in_specs, out_specs=out_specs, check_vma=False
    )
```

```python
import jax
import jax.numpy as jnp
from jax import lax
from jax.sharding import PartitionSpec as P
from jax.experimental import pallas as pl
from jax.experimental.pallas import tpu as pltpu

MESH = pl.DeviceIdType.MESH
HIGH = lax.Precision.HIGHEST
F32, BF16 = jnp.float32, jnp.bfloat16


def position():
    p, q = lax.axis_index("row"), lax.axis_index("col")
    return p, q, p // 8, p % 8, q // 8, (q // 2) % 4, q % 2


def device(zh, y, x, zl, c):
    return (zh * 8 + y, x * 8 + zl * 2 + c)


def send(src, dst, send_sem, recv_sem, target):
    return pltpu.make_async_remote_copy(
        src_ref=src, dst_ref=dst, send_sem=send_sem, recv_sem=recv_sem,
        device_id=target, device_id_type=MESH,
    )


def dot(a, b, ca, cb, precision=None):
    return lax.dot_general(
        a, b, (((ca,), (cb,)), ((), ())), precision=precision, preferred_element_type=F32
    )


def halves(a):
    high = a.astype(BF16)
    return high, (a - high.astype(F32)).astype(BF16)


def dot3(a, b, ca, cb):
    (ah, al), (bh, bl) = halves(a), halves(b)
    return dot(ah, bh, ca, cb) + (dot(ah, bl, ca, cb) + dot(al, bh, ca, cb))


def thirds(a):
    high = a.astype(BF16).astype(F32)
    rest = a - high
    middle = rest.astype(BF16).astype(F32)
    return high, middle, rest - middle


def outer(a, b):
    (ah, am, al), (bh, bm, bl) = thirds(a), thirds(b)
    left = jnp.concatenate([ah, ah, am, am, ah, al], 0).astype(BF16)
    right = jnp.concatenate([bh, bm, bh, bm, bl, bh], 0).astype(BF16)
    return dot(left, right, 0, 0)


def spread_columns(rows, base):
    turned = pltpu.roll(rows, (128 - base) % 128, 1)
    return [jnp.broadcast_to(turned[:, j : j + 1], (8, 128)) for j in range(8)]


def cholesky_block(k, a, ut):
    base = pl.multiple_of(8 * k, 8)
    sub = lax.broadcasted_iota(jnp.int32, (8, 128), 0)
    lane = lax.broadcasted_iota(jnp.int32, (8, 128), 1)
    rows = a[pl.ds(base, 8), :]
    cols = spread_columns(rows, base)
    for j in range(8):
        pivot = cols[j][j : j + 1]
        inv = lax.rsqrt(pivot)
        inv = inv * (1.5 - 0.5 * pivot * inv * inv)
        unit = rows[j : j + 1] * inv
        factor = jnp.where(sub > j, cols[j] * inv, 0.0)
        rows = jnp.where(sub == j, unit, rows - factor * unit)
        for i in range(j + 1, 8):
            cols[i] = cols[i] - factor * (cols[i][j : j + 1] * inv)
    done = jnp.where(lane >= base + sub, rows, 0.0)
    ut[pl.ds(base, 8), :] = done
    a[...] -= outer(done, done)


def inverse_block(k, n, t, lower, upper):
    base = pl.multiple_of(8 * k, 8)
    sub = lax.broadcasted_iota(jnp.int32, (8, 128), 0)
    rows, turned = n[pl.ds(base, 8), :], t[pl.ds(base, 8), :]
    rc, tc = spread_columns(rows[:, :128], base), spread_columns(turned[:, :128], base)
    scale = jnp.zeros((8, 128), F32)
    for j in range(8):
        inv = 1.0 / rc[j][j : j + 1]
        scale = jnp.where(sub == j, inv, scale)
        down = jnp.where(sub > j, rc[j] * inv, 0.0)
        across = jnp.where(sub > j, tc[j] * inv, 0.0)
        rows = rows - jnp.concatenate([down, down], 1) * rows[j : j + 1]
        turned = turned - jnp.concatenate([across, across], 1) * turned[j : j + 1]
        for i in range(j + 1, 8):
            rc[i] = rc[i] - down * rc[i][j : j + 1]
            tc[i] = tc[i] - across * tc[i][j : j + 1]
    turned = turned * jnp.concatenate([scale, scale], 1)
    lower[pl.ds(base, 8), :] = rows[:, 128:]
    upper[pl.ds(base, 8), :] = turned[:, 128:]
    n[...] -= outer(turned[:, :128], rows)
    t[...] -= outer(rows[:, :128], turned)


def step_kernel(psi, hpsi, counts, stored, out, bands, part, theirs, wa, wb, ra1, rb1, a1, b1, ra2,
                rb2, ab2, r3, own, srow, scol, mh, slr, slc, gram, cross, gx, gfull, s1, tops, m1c, m1r,
                raw, rawt, xt, tpart, xin, xown, xr, xc, work, ut, n, t, lower, upper, zr, zc, tx, tfull,
                load, ss, rs, ss_b, rs_b, ss_p, rs_p, ss_r, rs_r, ss_c, rs_c, ss_g, rs_g, ss_h, rs_h,
                ss_s, rs_s, ss_m, rs_m, ss_k, rs_k, ss_x, rs_x, ss_y, rs_y, ss_z, rs_z,
                ss_w, rs_w, ss_v, rs_v):
    p, q, zh, y, x, zl, c = position()
    z = zh * 4 + zl
    first = c == 0
    f = jnp.where(first, y, z)
    s = jnp.where(first, z, y)
    half, slot = q // 16, q % 16
    piece_at = q // 2
    row_slot = 16 * (q % 2) + q // 2
    home = p + 16 * (q % 2)
    at_home = home == q

    def at(xx, ff, sf):
        yy, zz = jnp.where(first, ff, sf), jnp.where(first, sf, ff)
        return device(zz // 4, yy, xx, zz % 4, c)

    def loop(start, stop, body):
        def step(i, carry):
            body(i)
            return carry
        lax.fori_loop(start, stop, step, 0)

    def fetch(g):
        xx = (x + 1 + g) % 4
        return pltpu.make_async_copy(
            psi.at[:, pl.ds(pl.multiple_of(2048 * xx, 2048), 2048)], bands.at[xx], load.at[g]
        )

    for g in range(4):
        fetch(g).start()

    partner = device(zh, y, x, zl, 1 - c)
    barrier = pltpu.get_barrier_semaphore()

    def hail(who):
        pl.semaphore_signal(barrier, inc=1, device_id=who, device_id_type=MESH)

    def hail_unless_me(who):
        @pl.when((who[0] != p) | (who[1] != q))
        def _():
            hail(who)

    hail(partner)
    for d in range(1, 4):
        hail(at((x + d) % 4, f, s))
    for d in range(1, 8):
        hail(at(x, (f + d) % 8, s))
        hail(at(x, f, (s + d) % 8))
    loop(1, 16, lambda d: hail(((p + d) % 16, q)))
    loop(1, 32, lambda d: hail((p, (q + d) % 32)))
    loop(0, 16, lambda j: hail_unless_me((slot, 2 * j + half)))

    live = lax.broadcasted_iota(jnp.int32, (256, 128), 0) < counts[0]
    panel = jnp.where(live, hpsi[...].astype(F32), 0.0).astype(BF16)
    raw[...] = stored[0]
    for h in range(2):
        for j in range(16):
            mh[16 * h + j] = stored[2 * j + h]

    in_rim = (q >= 8) & (q < 16)
    rim = jnp.clip(q - 8, 0, 7) // 2

    @pl.when(in_rim)
    def _():
        for h in range(2):
            rawt[h] = mh[16 * h : 16 * h + 16, :, :128].reshape(256, 128).T[:16]
        m1r[:, rim, c] = rawt[...]


    def multiply(g):
        xx = (x + 1 + g) % 4
        fetch(g).wait()

        def four(i):
            for u in range(4):
                at_chunk = pl.ds(pl.multiple_of(512 * i + 128 * u, 128), 128)
                part[xx, i, u // 2, u % 2] = dot(bands[xx, :, at_chunk], panel, 0, 0).reshape(8, 16, 128)

        loop(0, 4, four)

    def swap(g):
        xx = (x + 1 + g) % 4
        return send(part.at[xx, :, 1 - c], theirs.at[xx], ss_p.at[g], rs_p.at[g], partner)

    for g in range(3):
        multiply(g)
    pl.semaphore_wait(barrier, 18 + 15 + 31 + 15 + jnp.where(at_home, 0, 1))
    for g in range(3):
        swap(g).start()

    from_panel = jnp.maximum(p - 8, 0)

    def put_m(d):
        return send(raw, m1c.at[from_panel], ss_m.at[d], rs_m.at[from_panel], ((p + d) % 16, q))

    def put_k(d):
        return send(rawt, m1r.at[:, rim, c], ss_k.at[d], rs_k.at[rim], (p, (q + 2 * d) % 32))

    @pl.when(in_rim)
    def _():
        loop(1, 16, lambda d: put_k(d).start())

    @pl.when(p >= 8)
    def _():
        m1c[from_panel] = raw[...]
        loop(1, 16, lambda d: put_m(d).start())

    multiply(3)
    swap(3).start()

    def stage_a(g):
        xx = (x + 1 + g) % 4
        return send(wa.at[xx], ra1.at[g], ss.at[g], rs.at[g], at(xx, f, s))

    def stage_b(g, d):
        xx, ff = (x + 1 + g) % 4, (f + d) % 8
        return send(
            wb.at[ff, xx], rb1.at[d - 1, xx], ss_b.at[8 * g + d], rs_b.at[8 * g + d], at(x, ff, s)
        )

    for g in range(4):
        xx = (x + 1 + g) % 4
        swap(g).wait()

        def join(ff):
            for sf in range(8):
                yy, zz = jnp.where(first, ff, sf), jnp.where(first, sf, ff)
                hh, ll = zz // 4, zz % 4
                total = part[xx, ll, c, hh, yy] + theirs[xx, ll, hh, yy]
                wa[xx, ff, sf] = total[:8]
                wb[ff, xx, sf] = total[8:]

        loop(0, 8, join)
        if g < 3:
            stage_a(g).start()
        loop(1, 8, lambda d: stage_b(g, d).start())

    for g in range(4):
        loop(1, 8, lambda d: stage_b(g, d).wait())

    def sum_b1(i):
        total = wb[f, i]
        for d in range(7):
            total += rb1[d, i]
        b1[i] = total

    loop(0, 4, sum_b1)
    copies_b = []
    for d in range(1, 4):
        xx = (x + d) % 4
        copies_b.append(send(b1.at[xx], rb2.at[d - 1], ss.at[10 + d], rs.at[10 + d], at(xx, f, s)))
        copies_b[-1].start()
    for g in range(3):
        stage_a(g).wait()

    def sum_a1(i):
        total = wa[x, i]
        for d in range(3):
            total += ra1[d, i]
        a1[i] = total

    loop(0, 8, sum_a1)
    copies_a = []
    for d in range(1, 8):
        ff = (f + d) % 8
        copies_a.append(send(a1.at[ff], ra2.at[d - 1], ss.at[13 + d], rs.at[13 + d], at(x, ff, s)))
        copies_a[-1].start()
    for copy in copies_b:
        copy.wait()
    ab2[:, 1] = b1[x] + rb2[0] + rb2[1] + rb2[2]
    for copy in copies_a:
        copy.wait()
    total = a1[f]
    for d in range(7):
        total += ra2[d]
    ab2[:, 0] = total
    copies = []
    for d in range(1, 8):
        sf = (s + d) % 8
        copies.append(send(ab2.at[sf], r3.at[d - 1], ss.at[20 + d], rs.at[20 + d], at(x, f, sf)))
        copies[-1].start()
    for copy in copies:
        copy.wait()
    total = ab2[s]
    for d in range(7):
        total += r3[d]
    own[...] = total.reshape(16, 128)
    srow[row_slot] = own[...]

    def to_row_group(src, dst, sem, landed):
        return lambda d: send(src, dst, sem.at[d], landed, ((p + d) % 16, q))

    def to_col_group(src, dst, sem, landed):
        return lambda d: send(src, dst, sem.at[d], landed, (p, (q + d) % 32))

    def start_all(copy, stop):
        loop(1, stop, lambda d: copy(d).start())

    def sent_all(copy, stop):
        loop(1, stop, lambda d: copy(d).wait_send())

    def landed(dst, sem):
        send(dst, dst, ss.at[0], sem, (p, q)).wait_recv()

    put_r = to_col_group(own, srow.at[row_slot], ss_r, rs_r.at[row_slot])

    def put_c(d):
        return send(own, scol.at[q // 2], ss_c.at[d], rs_c.at[q // 2], ((p + d) % 16, home))

    start_all(put_c, 16)
    start_all(put_r, 32)

    @pl.when(at_home)
    def _():
        scol[q // 2] = own[...]

    @pl.when(jnp.logical_not(at_home))
    def _():
        put_c(0).start()

    relay = send(m1r.at[:, :, c], m1r.at[:, :, c], ss.at[28], rs.at[28], partner)

    def take_rim(i):
        @pl.when(8 + 2 * i + c != q)
        def _():
            landed(m1r.at[:, i, c], rs_k.at[i])

    loop(0, 4, take_rim)
    relay.start()

    def take_mc(i):
        @pl.when(i + 8 != p)
        def _():
            landed(m1c.at[i], rs_m.at[i])

    loop(0, 8, take_mc)
    def take_col(buffer, sem):
        def take(j):
            @pl.when((slot != p) | (2 * j + half != q))
            def _():
                landed(buffer.at[j], sem.at[j])

        loop(0, 16, take)

    def take_row(buffer, sem):
        def take(d):
            owner = (q + d) % 32
            at_slot = 16 * (owner % 2) + owner // 2
            landed(buffer.at[at_slot], sem.at[at_slot])

        loop(1, 32, take)

    take_row(srow, rs_r)
    relay.wait_recv()
    zero = jnp.zeros((16, 128), F32)
    slr[...] = srow[...]

    @pl.when(p < 8)
    def _():
        slr[0] = zero

    low = slr[...].reshape(512, 128)
    gram[...] = dot(low, low, 0, 0, HIGH)
    cross[...] = dot3(m1r[0].reshape(128, 256), low[:256], 1, 0) + dot3(
        m1r[1].reshape(128, 256), low[256:], 1, 0
    )
    at_piece = pl.ds(pl.multiple_of(8 * piece_at, 8), 8)
    gx[p, 0] = gram[at_piece, :]
    gx[p, 1] = cross[at_piece, :]
    put_g = to_row_group(gx.at[p], gx.at[p], ss_g, rs_g.at[p])
    start_all(put_g, 16)
    put_s = to_row_group(s1.at[from_panel], s1.at[from_panel], ss_s, rs_s.at[from_panel])

    @pl.when(p >= 8)
    def _():
        s1[from_panel, 0] = srow[0]
        s1[from_panel, 1] = m1r[0].reshape(128, 256)[:, :128].T[:16]
        start_all(put_s, 16)

    lane = lax.broadcasted_iota(jnp.int32, (16, 128), 1)
    in_left = (lane < 16) & (q < 8)

    @pl.when(q < 8)
    def _():
        left = pltpu.roll(srow[...].reshape(512, 128), (128 - 16 * (q % 8)) % 128, 1).reshape(32, 16, 128)
        mh[:, :, :128] = jnp.where(in_left[None], left, mh[:, :, :128])

    take_col(scol, rs_c)
    slc[...] = scol[...]

    @pl.when(q < 8)
    def _():
        slc[0] = zero

    @pl.when(p < 8)
    def _():
        turned = pltpu.roll(scol[...].reshape(256, 128), (128 - 16 * (p % 8)) % 128, 1)
        upper_rows = turned.T[:16]
        mh[0, :, :128] = jnp.where(
            in_left, 0.5 * (mh[0, :, :128] + upper_rows[:, :128]), upper_rows[:, :128]
        )
        mh[0, :, 128:] = upper_rows[:, 128:]

    xpart = dot3(mh[...].reshape(512, 256), slc[...].reshape(256, 128), 1, 0)
    xt[:, :16] = xpart.reshape(32, 16, 128)
    tpart[...] = dot3(low, xpart, 0, 0)

    def spread(i):
        xt[i, 16:] = tpart[pl.ds(pl.multiple_of(8 * (i % 16), 8), 8), :]

    loop(0, 32, spread)

    def put_x(d):
        to = (q + d) % 32
        return send(
            xt.at[16 * (to % 2) + to // 2], xin.at[q], ss_x.at[d], rs_x.at[q], (p, to)
        )

    start_all(put_x, 32)

    def all_landed(buffer, sem, count, me):
        loop(1, count, lambda d: landed(buffer.at[(me + d) % count], sem.at[(me + d) % count]))

    def total_of(buffer, count):
        total = buffer[0]
        for i in range(1, count):
            total += buffer[i]
        return total

    def put_piece(full, sem, got):
        def copy(d):
            to = (piece_at + d) % 16
            return send(full.at[piece_at], full.at[piece_at], sem.at[d], got.at[piece_at], (p, 2 * to + c))
        return copy

    all_landed(gx, rs_g, 16, p)
    gfull[piece_at] = total_of(gx, 16)
    put_h = put_piece(gfull, ss_h, rs_h)
    start_all(put_h, 16)

    all_landed(xin, rs_x, 32, q)
    xin[q] = xt[row_slot]
    both = total_of(xin, 32)
    xown[...] = both[:16]
    tx[p] = both[16:]
    xr[row_slot] = both[:16]
    put_w = to_row_group(tx.at[p], tx.at[p], ss_w, rs_w.at[p])
    start_all(put_w, 16)
    put_y = to_col_group(xown, xr.at[row_slot], ss_y, rs_y.at[row_slot])
    start_all(put_y, 32)

    def put_z(d):
        return send(xown, xc.at[q // 2], ss_z.at[d], rs_z.at[q // 2], ((p + d) % 16, home))

    start_all(put_z, 16)

    @pl.when(at_home)
    def _():
        xc[q // 2] = xown[...]

    @pl.when(jnp.logical_not(at_home))
    def _():
        put_z(0).start()

    all_landed(gfull, rs_h, 16, piece_at)
    gram_all = gfull[:, 0].reshape(128, 128)
    work[...] = gram_all
    loop(0, 16, lambda k: cholesky_block(k, work, ut))

    def take_from_panel(i):
        @pl.when(i + 8 != p)
        def _():
            landed(s1.at[i], rs_s.at[i])

    loop(0, 8, take_from_panel)
    tops[...] = s1[:, 0].reshape(128, 128)
    normal = gram_all - dot(ut[...], tops[...], 0, 0, HIGH)
    eye = (
        lax.broadcasted_iota(jnp.int32, (128, 128), 0) == lax.broadcasted_iota(jnp.int32, (128, 128), 1)
    ).astype(F32)
    n[:, :128] = normal
    n[:, 128:] = eye
    t[:, :128] = normal.T
    t[:, 128:] = eye
    all_landed(tx, rs_w, 16, p)
    tfull[piece_at] = total_of(tx, 16)
    put_v = put_piece(tfull, ss_v, rs_v)
    start_all(put_v, 16)
    loop(0, 16, lambda k: inverse_block(k, n, t, lower, upper))
    inverse_t = dot(lower[...], upper[...], 0, 0, HIGH)
    work[...] = inverse_t
    root = ut[...]
    turn = dot(gfull[:, 1].reshape(128, 128), root, 0, 0, HIGH)
    rest = dot(dot(root, s1[:, 1].reshape(128, 128), 0, 0, HIGH), root, 1, 0, HIGH) - (turn + turn.T)

    @pl.when(p >= 8)
    def _():
        slr[0] -= ut[pl.ds(pl.multiple_of(16 * from_panel, 16), 16), :]

    @pl.when((q >= 8) & (q < 16))
    def _():
        slc[0] -= ut[pl.ds(pl.multiple_of(16 * jnp.clip(q - 8, 0, 7), 16), 16), :]

    all_lanes = lax.broadcasted_iota(jnp.int32, (128, 128), 1)

    def patched(block, at_tile):
        fresh = pltpu.roll(tops[...], (128 - 16 * (at_tile % 8)) % 128, 1)
        return jnp.where((all_lanes < 16) & (at_tile < 8), fresh, block)

    rim0 = m1r[0].reshape(128, 256)
    rim0 = jnp.concatenate([patched(rim0[:, :128], p), rim0[:, 128:]], 1)
    rimc = m1c[...].reshape(128, 256)
    rimc = jnp.concatenate([patched(rimc[:, :128], q), rimc[:, 128:]], 1)
    zr[...] = jnp.concatenate(
        [dot3(rim0, root, 0, 0), dot3(m1r[1].reshape(128, 256), root, 0, 0)], 0
    )
    zc[...] = dot3(rimc, root, 0, 0)
    take_row(xr, rs_y)
    take_col(xc, rs_z)
    acols = dot3(xc[...].reshape(256, 128) - zc[...], work[...], 1, 0)
    ycols = slc[...].reshape(256, 128)
    rh, rl = halves(jnp.concatenate([acols, ycols], 1))
    for h in range(4):
        rows = slr[pl.ds(8 * h, 8)].reshape(128, 128)
        brows = dot3(
            xr[pl.ds(8 * h, 8)].reshape(128, 128) - zr[pl.ds(128 * h, 128), :], work[...], 1, 0
        )
        lh, ll = halves(jnp.concatenate([rows, brows], 1))
        change = dot(lh, rh, 1, 1) + (dot(lh, rl, 1, 1) + dot(ll, rh, 1, 1))
        mh[pl.ds(8 * h, 8)] = mh[pl.ds(8 * h, 8)] - change.reshape(8, 16, 256)
    all_landed(tfull, rs_v, 16, piece_at)
    wmat = tfull[...].reshape(128, 128) + rest
    core = dot(dot(work[...], wmat, 0, 0, HIGH), work[...], 1, 0, HIGH)
    ch, cl = halves(dot3(ycols, core, 1, 1))
    for h in range(4):
        lh, ll = halves(slr[pl.ds(8 * h, 8)].reshape(128, 128))
        change = dot(lh, ch, 1, 1) + (dot(lh, cl, 1, 1) + dot(ll, ch, 1, 1))
        for i in range(8):
            at_tile = 8 * h + i
            out[2 * (at_tile % 16) + at_tile // 16] = mh[at_tile] + change[16 * i : 16 * i + 16]

    sent_all(put_c, 16)
    sent_all(put_r, 32)
    sent_all(put_g, 16)
    sent_all(put_h, 16)
    sent_all(put_x, 32)
    sent_all(put_y, 32)
    sent_all(put_z, 16)
    sent_all(put_w, 16)
    sent_all(put_v, 16)

    relay.wait_send()

    @pl.when(jnp.logical_not(at_home))
    def _():
        put_c(0).wait_send()
        put_z(0).wait_send()

    @pl.when(p >= 8)
    def _():
        sent_all(put_s, 16)
        sent_all(put_m, 16)

    @pl.when(in_rim)
    def _():
        sent_all(put_k, 16)


def step(psi, hpsi, counts, stored):
    vmem = pl.BlockSpec(memory_space=pltpu.VMEM)

    def room(*dims):
        return pltpu.VMEM(dims, F32)

    sems = [4, 32, 32, 32, 32, 4, 4, 32, 32, 16, 16, 16, 16, 16, 16, 16, 8, 16, 8, 16, 16, 32, 32, 32, 32, 16, 16, 16, 16, 16, 16]
    return pl.pallas_call(
        step_kernel,
        name="step",
        out_shape=jax.ShapeDtypeStruct((32, 16, 256), F32),
        in_specs=[pl.BlockSpec(memory_space=pltpu.HBM), vmem, pl.BlockSpec(memory_space=pltpu.SMEM), vmem],
        out_specs=vmem,
        scratch_shapes=[
            pltpu.VMEM((4, 256, 2048), BF16), room(4, 4, 2, 2, 8, 16, 128),
            room(4, 4, 2, 8, 16, 128), room(4, 8, 8, 8, 128), room(8, 4, 8, 8, 128),
            room(3, 8, 8, 8, 128), room(7, 4, 8, 8, 128), room(8, 8, 8, 128), room(4, 8, 8, 128),
            room(7, 8, 8, 128), room(3, 8, 8, 128), room(8, 2, 8, 128), room(7, 2, 8, 128),
            room(16, 128),
            room(32, 16, 128), room(16, 16, 128), room(32, 16, 256), room(32, 16, 128),
            room(16, 16, 128), room(128, 128), room(128, 128), room(16, 2, 8, 128),
            room(16, 2, 8, 128), room(8, 2, 16, 128), room(128, 128), room(8, 16, 256),
            room(2, 4, 2, 16, 256), room(16, 256), room(2, 16, 256), room(32, 24, 128), room(128, 128),
            room(32, 24, 128), room(16, 128), room(32, 16, 128), room(16, 16, 128),
            room(128, 128), room(128, 128), room(128, 256), room(128, 256), room(128, 128),
            room(128, 128), room(512, 128), room(256, 128), room(16, 8, 128), room(16, 8, 128),
        ] + [pltpu.SemaphoreType.DMA((k,)) for k in sems],
        compiler_params=pltpu.CompilerParams(
            collective_id=1, has_side_effects=True, vmem_limit_bytes=62 << 20
        ),
    )(psi, hpsi, counts, stored)


def per_device(psi, hpsi, slab_counts, matrix):
    return step(psi, hpsi, slab_counts, matrix.reshape(32, 16, 256)).reshape(matrix.shape)


def solution(mesh):
    in_specs = (
        P(("row", "col"), None),
        P(("row", "col"), None),
        P(("row", "col")),
        P("row", None, "col", None),
    )
    out_specs = P("row", None, "col", None)
    return jax.shard_map(
        per_device, mesh=mesh, in_specs=in_specs, out_specs=out_specs, check_vma=False
    )
```

```python
import jax
import jax.numpy as jnp
from jax import lax
from jax.sharding import PartitionSpec as P
from jax.experimental import pallas as pl
from jax.experimental.pallas import tpu as pltpu

MESH = pl.DeviceIdType.MESH
HIGH = lax.Precision.HIGHEST
BLOCK = 16
F32, BF16 = jnp.float32, jnp.bfloat16


def position():
    p, q = lax.axis_index("row"), lax.axis_index("col")
    return p, q, p // 8, p % 8, q // 8, (q // 2) % 4, q % 2


def device(zh, y, x, zl, c):
    return (zh * 8 + y, x * 8 + zl * 2 + c)


def send(src, dst, send_sem, recv_sem, target):
    return pltpu.make_async_remote_copy(
        src_ref=src, dst_ref=dst, send_sem=send_sem, recv_sem=recv_sem,
        device_id=target, device_id_type=MESH,
    )


def dot(a, b, ca, cb, precision=None):
    return lax.dot_general(
        a, b, (((ca,), (cb,)), ((), ())), precision=precision, preferred_element_type=F32
    )


def halves(a):
    high = a.astype(BF16)
    return high, (a - high.astype(F32)).astype(BF16)


def dot3(a, b, ca, cb):
    (ah, al), (bh, bl) = halves(a), halves(b)
    return dot(ah, bh, ca, cb) + (dot(ah, bl, ca, cb) + dot(al, bh, ca, cb))


def thirds(a):
    high = a.astype(BF16).astype(F32)
    rest = a - high
    middle = rest.astype(BF16).astype(F32)
    return high, middle, rest - middle


def outer(a, b):
    (ah, am, al), (bh, bm, bl) = thirds(a), thirds(b)
    left = jnp.concatenate([ah, ah, am, am, ah, al], 0).astype(BF16)
    right = jnp.concatenate([bh, bm, bh, bm, bl, bh], 0).astype(BF16)
    return dot(left, right, 0, 0)


def spread_columns(rows, base):
    turned = pltpu.roll(rows, (128 - base) % 128, 1)
    return [jnp.broadcast_to(turned[:, j : j + 1], (BLOCK, 128)) for j in range(BLOCK)]


def cholesky_block(k, a, ut):
    base = pl.multiple_of(BLOCK * k, BLOCK)
    sub = lax.broadcasted_iota(jnp.int32, (BLOCK, 128), 0)
    lane = lax.broadcasted_iota(jnp.int32, (BLOCK, 128), 1)
    rows = a[pl.ds(base, BLOCK), :]
    cols = spread_columns(rows, base)
    for j in range(BLOCK):
        pivot = cols[j][j : j + 1]
        inv = lax.rsqrt(pivot)
        inv = inv * (1.5 - 0.5 * pivot * inv * inv)
        unit = rows[j : j + 1] * inv
        factor = jnp.where(sub > j, cols[j] * inv, 0.0)
        rows = jnp.where(sub == j, unit, rows - factor * unit)
        for i in range(j + 1, BLOCK):
            cols[i] = cols[i] - factor * (cols[i][j : j + 1] * inv)
    done = jnp.where(lane >= base + sub, rows, 0.0)
    ut[pl.ds(base, BLOCK), :] = done
    a[...] -= outer(done, done)


def inverse_block(k, n, t, lower, upper):
    base = pl.multiple_of(BLOCK * k, BLOCK)
    sub = lax.broadcasted_iota(jnp.int32, (BLOCK, 128), 0)
    rows, turned = n[pl.ds(base, BLOCK), :], t[pl.ds(base, BLOCK), :]
    rc, tc = spread_columns(rows[:, :128], base), spread_columns(turned[:, :128], base)
    scale = jnp.zeros((BLOCK, 128), F32)
    for j in range(BLOCK):
        inv = 1.0 / rc[j][j : j + 1]
        scale = jnp.where(sub == j, inv, scale)
        down = jnp.where(sub > j, rc[j] * inv, 0.0)
        across = jnp.where(sub > j, tc[j] * inv, 0.0)
        rows = rows - jnp.concatenate([down, down], 1) * rows[j : j + 1]
        turned = turned - jnp.concatenate([across, across], 1) * turned[j : j + 1]
        for i in range(j + 1, BLOCK):
            rc[i] = rc[i] - down * rc[i][j : j + 1]
            tc[i] = tc[i] - across * tc[i][j : j + 1]
    turned = turned * jnp.concatenate([scale, scale], 1)
    lower[pl.ds(base, BLOCK), :] = rows[:, 128:]
    upper[pl.ds(base, BLOCK), :] = turned[:, 128:]
    n[...] -= outer(turned[:, :128], rows)
    t[...] -= outer(rows[:, :128], turned)


def step_kernel(psi, hpsi, counts, stored, out, bands, part, theirs, wa, wb, ra1, rb1, a1, b1, ra2,
                rb2, ab2, r3, own, srow, scol, mh, slr, slc, gram, cross, gx, gfull, s1, tops, m1c, m1r,
                raw, rawt, xt, xo, xsum, tpart, xin, xown, xr, xc, work, ut, n, t, lower, upper, zr, zc, tx, tfull,
                load, ss, rs, ss_b, rs_b, ss_p, rs_p, ss_r, rs_r, ss_c, rs_c, ss_g, rs_g, ss_h, rs_h,
                ss_s, rs_s, ss_m, rs_m, ss_k, rs_k, ss_x, rs_x, ss_y, rs_y, ss_z, rs_z,
                ss_w, rs_w, ss_v, rs_v):
    p, q, zh, y, x, zl, c = position()
    z = zh * 4 + zl
    first = c == 0
    f = jnp.where(first, y, z)
    s = jnp.where(first, z, y)
    half, slot = q // 16, q % 16
    piece_at = q // 2
    row_slot = 16 * (q % 2) + q // 2
    home = p + 16 * (q % 2)
    at_home = home == q

    def at(xx, ff, sf):
        yy, zz = jnp.where(first, ff, sf), jnp.where(first, sf, ff)
        return device(zz // 4, yy, xx, zz % 4, c)

    def loop(start, stop, body):
        def step(i, carry):
            body(i)
            return carry
        lax.fori_loop(start, stop, step, 0)

    def fetch(g):
        xx = (x + 1 + g) % 4
        return pltpu.make_async_copy(
            psi.at[:, pl.ds(pl.multiple_of(2048 * xx, 2048), 2048)], bands.at[xx], load.at[g]
        )

    for g in range(4):
        fetch(g).start()

    partner = device(zh, y, x, zl, 1 - c)
    barrier = pltpu.get_barrier_semaphore()

    def hail(who):
        pl.semaphore_signal(barrier, inc=1, device_id=who, device_id_type=MESH)

    def hail_unless_me(who):
        @pl.when((who[0] != p) | (who[1] != q))
        def _():
            hail(who)

    hail(partner)
    for d in range(1, 4):
        hail(at((x + d) % 4, f, s))
    for d in range(1, 8):
        hail(at(x, (f + d) % 8, s))
        hail(at(x, f, (s + d) % 8))
    loop(1, 16, lambda d: hail(((p + d) % 16, q)))
    loop(1, 32, lambda d: hail((p, (q + d) % 32)))
    loop(0, 16, lambda j: hail_unless_me((slot, 2 * j + half)))

    live = lax.broadcasted_iota(jnp.int32, (256, 128), 0) < counts[0]
    panel = jnp.where(live, hpsi[...].astype(F32), 0.0).astype(BF16)
    def halves_of(i):
        return [pl.ds(32 * i + k, 16, stride=2) for k in range(2)]

    for h in range(2):
        for j in range(16):
            for k, lines in enumerate(halves_of(2 * j + h)):
                mh[16 * h + j, :, 128 * k : 128 * k + 128] = stored[lines, :]

    raw[...] = mh[0]
    in_rim = (q >= 8) & (q < 16)
    rim = jnp.clip(q - 8, 0, 7) // 2

    @pl.when(in_rim)
    def _():
        for h in range(2):
            rawt[h] = mh[16 * h : 16 * h + 16, :, :128].reshape(256, 128).T[:16]
        m1r[:, rim, c] = rawt[...]


    def multiply(g):
        xx = (x + 1 + g) % 4
        fetch(g).wait()

        def four(i):
            for u in range(4):
                at_chunk = pl.ds(pl.multiple_of(512 * i + 128 * u, 128), 128)
                part[xx, i, u // 2, u % 2] = dot(bands[xx, :, at_chunk], panel, 0, 0).reshape(8, 16, 128)

        loop(0, 4, four)

    def swap(g):
        xx = (x + 1 + g) % 4
        return send(part.at[xx, :, 1 - c], theirs.at[xx], ss_p.at[g], rs_p.at[g], partner)

    for g in range(3):
        multiply(g)
    pl.semaphore_wait(barrier, 18 + 15 + 31 + 15 + jnp.where(at_home, 0, 1))
    for g in range(3):
        swap(g).start()

    from_panel = jnp.maximum(p - 8, 0)

    def put_m(d):
        return send(raw, m1c.at[from_panel], ss_m.at[d], rs_m.at[from_panel], ((p + d) % 16, q))

    def put_k(d):
        return send(rawt, m1r.at[:, rim, c], ss_k.at[d], rs_k.at[rim], (p, (q + 2 * d) % 32))

    @pl.when(in_rim)
    def _():
        loop(1, 16, lambda d: put_k(d).start())

    @pl.when(p >= 8)
    def _():
        m1c[from_panel] = raw[...]
        loop(1, 16, lambda d: put_m(d).start())

    multiply(3)
    swap(3).start()

    def stage_a(g):
        xx = (x + 1 + g) % 4
        return send(wa.at[xx], ra1.at[g], ss.at[g], rs.at[g], at(xx, f, s))

    def stage_b(g, d):
        xx, ff = (x + 1 + g) % 4, (f + d) % 8
        return send(
            wb.at[ff, xx], rb1.at[d - 1, xx], ss_b.at[8 * g + d], rs_b.at[8 * g + d], at(x, ff, s)
        )

    for g in range(4):
        xx = (x + 1 + g) % 4
        swap(g).wait()

        def join(ff):
            for sf in range(8):
                yy, zz = jnp.where(first, ff, sf), jnp.where(first, sf, ff)
                hh, ll = zz // 4, zz % 4
                total = part[xx, ll, c, hh, yy] + theirs[xx, ll, hh, yy]
                wa[xx, ff, sf] = total[:8]
                wb[ff, xx, sf] = total[8:]

        loop(0, 8, join)
        if g < 3:
            stage_a(g).start()
        loop(1, 8, lambda d: stage_b(g, d).start())

    for g in range(4):
        loop(1, 8, lambda d: stage_b(g, d).wait())

    def sum_b1(i):
        total = wb[f, i]
        for d in range(7):
            total += rb1[d, i]
        b1[i] = total

    loop(0, 4, sum_b1)
    copies_b = []
    for d in range(1, 4):
        xx = (x + d) % 4
        copies_b.append(send(b1.at[xx], rb2.at[d - 1], ss.at[10 + d], rs.at[10 + d], at(xx, f, s)))
        copies_b[-1].start()
    for g in range(3):
        stage_a(g).wait()

    def sum_a1(i):
        total = wa[x, i]
        for d in range(3):
            total += ra1[d, i]
        a1[i] = total

    loop(0, 8, sum_a1)
    copies_a = []
    for d in range(1, 8):
        ff = (f + d) % 8
        copies_a.append(send(a1.at[ff], ra2.at[d - 1], ss.at[13 + d], rs.at[13 + d], at(x, ff, s)))
        copies_a[-1].start()
    for copy in copies_b:
        copy.wait()
    ab2[:, 1] = b1[x] + rb2[0] + rb2[1] + rb2[2]
    for copy in copies_a:
        copy.wait()
    total = a1[f]
    for d in range(7):
        total += ra2[d]
    ab2[:, 0] = total
    copies = []
    for d in range(1, 8):
        sf = (s + d) % 8
        copies.append(send(ab2.at[sf], r3.at[d - 1], ss.at[20 + d], rs.at[20 + d], at(x, f, sf)))
        copies[-1].start()
    for copy in copies:
        copy.wait()
    total = ab2[s]
    for d in range(7):
        total += r3[d]
    own[...] = total.reshape(16, 128)
    srow[row_slot] = own[...]

    def to_row_group(src, dst, sem, landed):
        return lambda d: send(src, dst, sem.at[d], landed, ((p + d) % 16, q))

    def to_col_group(src, dst, sem, landed):
        return lambda d: send(src, dst, sem.at[d], landed, (p, (q + d) % 32))

    def start_all(copy, stop):
        loop(1, stop, lambda d: copy(d).start())

    def sent_all(copy, stop):
        loop(1, stop, lambda d: copy(d).wait_send())

    def landed(dst, sem):
        send(dst, dst, ss.at[0], sem, (p, q)).wait_recv()

    put_r = to_col_group(own, srow.at[row_slot], ss_r, rs_r.at[row_slot])

    def put_c(d):
        return send(own, scol.at[q // 2], ss_c.at[d], rs_c.at[q // 2], ((p + d) % 16, home))

    start_all(put_c, 16)
    start_all(put_r, 32)

    @pl.when(at_home)
    def _():
        scol[q // 2] = own[...]

    @pl.when(jnp.logical_not(at_home))
    def _():
        put_c(0).start()

    relay = send(m1r.at[:, :, c], m1r.at[:, :, c], ss.at[28], rs.at[28], partner)

    def take_rim(i):
        @pl.when(8 + 2 * i + c != q)
        def _():
            landed(m1r.at[:, i, c], rs_k.at[i])

    loop(0, 4, take_rim)
    relay.start()

    def take_mc(i):
        @pl.when(i + 8 != p)
        def _():
            landed(m1c.at[i], rs_m.at[i])

    loop(0, 8, take_mc)
    def take_col(buffer, sem):
        def take(j):
            @pl.when((slot != p) | (2 * j + half != q))
            def _():
                landed(buffer.at[j], sem.at[j])

        loop(0, 16, take)

    def take_row(buffer, sem):
        def take(d):
            owner = (q + d) % 32
            at_slot = 16 * (owner % 2) + owner // 2
            landed(buffer.at[at_slot], sem.at[at_slot])

        loop(1, 32, take)

    take_row(srow, rs_r)
    relay.wait_recv()
    zero = jnp.zeros((16, 128), F32)
    slr[...] = srow[...]

    @pl.when(p < 8)
    def _():
        slr[0] = zero

    low = slr[...].reshape(512, 128)
    gram[...] = dot(low, low, 0, 0, HIGH)
    cross[...] = dot3(m1r[0].reshape(128, 256), low[:256], 1, 0) + dot3(
        m1r[1].reshape(128, 256), low[256:], 1, 0
    )
    at_piece = pl.ds(pl.multiple_of(8 * piece_at, 8), 8)
    gx[p, 0] = gram[at_piece, :]
    gx[p, 1] = cross[at_piece, :]
    put_g = to_row_group(gx.at[p], gx.at[p], ss_g, rs_g.at[p])
    start_all(put_g, 16)
    put_s = to_row_group(s1.at[from_panel], s1.at[from_panel], ss_s, rs_s.at[from_panel])

    @pl.when(p >= 8)
    def _():
        s1[from_panel, 0] = srow[0]
        s1[from_panel, 1] = m1r[0].reshape(128, 256)[:, :128].T[:16]
        start_all(put_s, 16)

    lane = lax.broadcasted_iota(jnp.int32, (16, 128), 1)
    in_left = (lane < 16) & (q < 8)

    @pl.when(q < 8)
    def _():
        left = pltpu.roll(srow[...].reshape(512, 128), (128 - 16 * (q % 8)) % 128, 1).reshape(32, 16, 128)
        mh[:, :, :128] = jnp.where(in_left[None], left, mh[:, :, :128])

    take_col(scol, rs_c)
    slc[...] = scol[...]

    @pl.when(q < 8)
    def _():
        slc[0] = zero

    @pl.when(p < 8)
    def _():
        turned = pltpu.roll(scol[...].reshape(256, 128), (128 - 16 * (p % 8)) % 128, 1)
        upper_rows = turned.T[:16]
        mh[0, :, :128] = jnp.where(
            in_left, 0.5 * (mh[0, :, :128] + upper_rows[:, :128]), upper_rows[:, :128]
        )
        mh[0, :, 128:] = upper_rows[:, 128:]

    xpart = dot3(mh[...].reshape(512, 256), slc[...].reshape(256, 128), 1, 0)
    xt[:, :, :16] = xpart.reshape(2, 16, 16, 128)
    tpart[...] = dot3(low, xpart, 0, 0)
    for h in range(2):
        xt[h, :, 16:] = tpart[...].reshape(16, 8, 128)
    pair = send(xt.at[1 - c], xo, ss.at[29], rs.at[29], partner)
    pair.start()
    pair.wait()
    xsum[...] = xt[c] + xo[...]

    def put_x(d):
        to = (piece_at + d) % 16
        return send(xsum.at[to], xin.at[piece_at], ss_x.at[d], rs_x.at[piece_at], (p, 2 * to + c))

    start_all(put_x, 16)

    sent_all(put_r, 32)
    sent_all(put_c, 16)

    @pl.when(jnp.logical_not(at_home))
    def _():
        put_c(0).wait_send()

    @pl.when(p >= 8)
    def _():
        sent_all(put_m, 16)

    @pl.when(in_rim)
    def _():
        sent_all(put_k, 16)

    def all_landed(buffer, sem, count, me):
        loop(1, count, lambda d: landed(buffer.at[(me + d) % count], sem.at[(me + d) % count]))

    def total_of(buffer, count):
        total = buffer[0]
        for i in range(1, count):
            total += buffer[i]
        return total

    def put_piece(full, sem, got):
        def copy(d):
            to = (piece_at + d) % 16
            return send(full.at[piece_at], full.at[piece_at], sem.at[d], got.at[piece_at], (p, 2 * to + c))
        return copy

    all_landed(gx, rs_g, 16, p)
    gfull[piece_at] = total_of(gx, 16)
    put_h = put_piece(gfull, ss_h, rs_h)
    start_all(put_h, 16)

    all_landed(xin, rs_x, 16, piece_at)
    xin[piece_at] = xsum[piece_at]
    both = total_of(xin, 16)
    xown[...] = both[:16]
    tx[p] = both[16:]
    xr[row_slot] = both[:16]
    put_w = to_row_group(tx.at[p], tx.at[p], ss_w, rs_w.at[p])
    start_all(put_w, 16)
    put_y = to_col_group(xown, xr.at[row_slot], ss_y, rs_y.at[row_slot])
    start_all(put_y, 32)

    def put_z(d):
        return send(xown, xc.at[q // 2], ss_z.at[d], rs_z.at[q // 2], ((p + d) % 16, home))

    start_all(put_z, 16)

    @pl.when(at_home)
    def _():
        xc[q // 2] = xown[...]

    @pl.when(jnp.logical_not(at_home))
    def _():
        put_z(0).start()

    sent_all(put_g, 16)
    sent_all(put_x, 16)

    @pl.when(p >= 8)
    def _():
        sent_all(put_s, 16)

    all_landed(gfull, rs_h, 16, piece_at)
    gram_all = gfull[:, 0].reshape(128, 128)
    work[...] = gram_all
    loop(0, 128 // BLOCK, lambda k: cholesky_block(k, work, ut))

    def take_from_panel(i):
        @pl.when(i + 8 != p)
        def _():
            landed(s1.at[i], rs_s.at[i])

    loop(0, 8, take_from_panel)
    tops[...] = s1[:, 0].reshape(128, 128)
    normal = gram_all - dot(ut[...], tops[...], 0, 0, HIGH)
    eye = (
        lax.broadcasted_iota(jnp.int32, (128, 128), 0) == lax.broadcasted_iota(jnp.int32, (128, 128), 1)
    ).astype(F32)
    n[:, :128] = normal
    n[:, 128:] = eye
    t[:, :128] = normal.T
    t[:, 128:] = eye
    loop(0, 3, lambda k: inverse_block(k, n, t, lower, upper))
    all_landed(tx, rs_w, 16, p)
    tfull[piece_at] = total_of(tx, 16)
    put_v = put_piece(tfull, ss_v, rs_v)
    start_all(put_v, 16)
    loop(3, 128 // BLOCK, lambda k: inverse_block(k, n, t, lower, upper))
    inverse_t = dot(lower[...], upper[...], 0, 0, HIGH)
    work[...] = inverse_t
    root = ut[...]
    turn = dot(gfull[:, 1].reshape(128, 128), root, 0, 0, HIGH)
    rest = dot(dot(root, s1[:, 1].reshape(128, 128), 0, 0, HIGH), root, 1, 0, HIGH) - (turn + turn.T)

    @pl.when(p >= 8)
    def _():
        slr[0] -= ut[pl.ds(pl.multiple_of(16 * from_panel, 16), 16), :]

    @pl.when((q >= 8) & (q < 16))
    def _():
        slc[0] -= ut[pl.ds(pl.multiple_of(16 * jnp.clip(q - 8, 0, 7), 16), 16), :]

    all_lanes = lax.broadcasted_iota(jnp.int32, (128, 128), 1)

    def patched(block, at_tile):
        fresh = pltpu.roll(tops[...], (128 - 16 * (at_tile % 8)) % 128, 1)
        return jnp.where((all_lanes < 16) & (at_tile < 8), fresh, block)

    rim0 = m1r[0].reshape(128, 256)
    rim0 = jnp.concatenate([patched(rim0[:, :128], p), rim0[:, 128:]], 1)
    rimc = m1c[...].reshape(128, 256)
    rimc = jnp.concatenate([patched(rimc[:, :128], q), rimc[:, 128:]], 1)
    zr[...] = jnp.concatenate(
        [dot3(rim0, root, 0, 0), dot3(m1r[1].reshape(128, 256), root, 0, 0)], 0
    )
    zc[...] = dot3(rimc, root, 0, 0)
    take_row(xr, rs_y)
    take_col(xc, rs_z)
    acols = dot3(xc[...].reshape(256, 128) - zc[...], work[...], 1, 0)
    ycols = slc[...].reshape(256, 128)
    rh, rl = halves(jnp.concatenate([acols, ycols], 1))
    for h in range(4):
        rows = slr[pl.ds(8 * h, 8)].reshape(128, 128)
        brows = dot3(
            xr[pl.ds(8 * h, 8)].reshape(128, 128) - zr[pl.ds(128 * h, 128), :], work[...], 1, 0
        )
        lh, ll = halves(jnp.concatenate([rows, brows], 1))
        change = dot(lh, rh, 1, 1) + (dot(lh, rl, 1, 1) + dot(ll, rh, 1, 1))
        mh[pl.ds(8 * h, 8)] = mh[pl.ds(8 * h, 8)] - change.reshape(8, 16, 256)
    sent_all(put_h, 16)
    sent_all(put_y, 32)
    sent_all(put_z, 16)
    sent_all(put_w, 16)

    @pl.when(jnp.logical_not(at_home))
    def _():
        put_z(0).wait_send()

    all_landed(tfull, rs_v, 16, piece_at)
    wmat = tfull[...].reshape(128, 128) + rest
    core = dot(dot(work[...], wmat, 0, 0, HIGH), work[...], 1, 0, HIGH)
    ch, cl = halves(dot3(ycols, core, 1, 1))
    for h in range(4):
        lh, ll = halves(slr[pl.ds(8 * h, 8)].reshape(128, 128))
        change = dot(lh, ch, 1, 1) + (dot(lh, cl, 1, 1) + dot(ll, ch, 1, 1))
        for i in range(8):
            at_tile = 8 * h + i
            tile = mh[at_tile] + change[16 * i : 16 * i + 16]
            for k, lines in enumerate(halves_of(2 * (at_tile % 16) + at_tile // 16)):
                out[lines, :] = tile[:, 128 * k : 128 * k + 128]

    sent_all(put_v, 16)
    relay.wait_send()


def step(psi, hpsi, counts, stored):
    vmem = pl.BlockSpec(memory_space=pltpu.VMEM)

    def room(*dims):
        return pltpu.VMEM(dims, F32)

    sems = [4, 32, 32, 32, 32, 4, 4, 32, 32, 16, 16, 16, 16, 16, 16, 16, 8, 16, 8, 16, 16, 32, 32, 32, 32, 16, 16, 16, 16, 16, 16]
    return pl.pallas_call(
        step_kernel,
        name="step",
        out_shape=jax.ShapeDtypeStruct((1024, 128), F32),
        in_specs=[pl.BlockSpec(memory_space=pltpu.HBM), vmem, pl.BlockSpec(memory_space=pltpu.SMEM), vmem],
        out_specs=vmem,
        scratch_shapes=[
            pltpu.VMEM((4, 256, 2048), BF16), room(4, 4, 2, 2, 8, 16, 128),
            room(4, 4, 2, 8, 16, 128), room(4, 8, 8, 8, 128), room(8, 4, 8, 8, 128),
            room(3, 8, 8, 8, 128), room(7, 4, 8, 8, 128), room(8, 8, 8, 128), room(4, 8, 8, 128),
            room(7, 8, 8, 128), room(3, 8, 8, 128), room(8, 2, 8, 128), room(7, 2, 8, 128),
            room(16, 128),
            room(32, 16, 128), room(16, 16, 128), room(32, 16, 256), room(32, 16, 128),
            room(16, 16, 128), room(128, 128), room(128, 128), room(16, 2, 8, 128),
            room(16, 2, 8, 128), room(8, 2, 16, 128), room(128, 128), room(8, 16, 256),
            room(2, 4, 2, 16, 256), room(16, 256), room(2, 16, 256), room(2, 16, 24, 128), room(16, 24, 128), room(16, 24, 128), room(128, 128),
            room(16, 24, 128), room(16, 128), room(32, 16, 128), room(16, 16, 128),
            room(128, 128), room(128, 128), room(128, 256), room(128, 256), room(128, 128),
            room(128, 128), room(512, 128), room(256, 128), room(16, 8, 128), room(16, 8, 128),
        ] + [pltpu.SemaphoreType.DMA((k,)) for k in sems],
        compiler_params=pltpu.CompilerParams(
            collective_id=1, has_side_effects=True, vmem_limit_bytes=62 << 20
        ),
    )(psi, hpsi, counts, stored)


def per_device(psi, hpsi, slab_counts, matrix):
    return step(psi, hpsi, slab_counts, matrix.reshape(1024, 128)).reshape(matrix.shape)


def solution(mesh):
    in_specs = (
        P(("row", "col"), None),
        P(("row", "col"), None),
        P(("row", "col")),
        P("row", None, "col", None),
    )
    out_specs = P("row", None, "col", None)
    return jax.shard_map(
        per_device, mesh=mesh, in_specs=in_specs, out_specs=out_specs, check_vma=False
    )
```

```python
import jax
import jax.numpy as jnp
from jax import lax
from jax.sharding import PartitionSpec as P
from jax.experimental import pallas as pl
from jax.experimental.pallas import tpu as pltpu

MESH = pl.DeviceIdType.MESH
HIGH = lax.Precision.HIGHEST
BLOCK = 16
F32, BF16 = jnp.float32, jnp.bfloat16


def position():
    p, q = lax.axis_index("row"), lax.axis_index("col")
    return p, q, p // 8, p % 8, q // 8, (q // 2) % 4, q % 2


def device(zh, y, x, zl, c):
    return (zh * 8 + y, x * 8 + zl * 2 + c)


def send(src, dst, send_sem, recv_sem, target):
    return pltpu.make_async_remote_copy(
        src_ref=src, dst_ref=dst, send_sem=send_sem, recv_sem=recv_sem,
        device_id=target, device_id_type=MESH,
    )


def dot(a, b, ca, cb, precision=None):
    return lax.dot_general(
        a, b, (((ca,), (cb,)), ((), ())), precision=precision, preferred_element_type=F32
    )


def halves(a):
    high = a.astype(BF16)
    return high, (a - high.astype(F32)).astype(BF16)


def dot3(a, b, ca, cb):
    (ah, al), (bh, bl) = halves(a), halves(b)
    return dot(ah, bh, ca, cb) + (dot(ah, bl, ca, cb) + dot(al, bh, ca, cb))


def thirds(a):
    high = a.astype(BF16).astype(F32)
    rest = a - high
    middle = rest.astype(BF16).astype(F32)
    return high, middle, rest - middle


def outer(a, b):
    (ah, am, al), (bh, bm, bl) = thirds(a), thirds(b)
    left = jnp.concatenate([ah, ah, am, am, ah, al], 0).astype(BF16)
    right = jnp.concatenate([bh, bm, bh, bm, bl, bh], 0).astype(BF16)
    return dot(left, right, 0, 0)


def spread_columns(rows, base):
    turned = pltpu.roll(rows, (128 - base) % 128, 1)
    return [jnp.broadcast_to(turned[:, j : j + 1], (BLOCK, 128)) for j in range(BLOCK)]


def cholesky_block(k, a, ut):
    base = pl.multiple_of(BLOCK * k, BLOCK)
    sub = lax.broadcasted_iota(jnp.int32, (BLOCK, 128), 0)
    lane = lax.broadcasted_iota(jnp.int32, (BLOCK, 128), 1)
    rows = a[pl.ds(base, BLOCK), :]
    cols = spread_columns(rows, base)
    for j in range(BLOCK):
        pivot = cols[j][j : j + 1]
        inv = lax.rsqrt(pivot)
        inv = inv * (1.5 - 0.5 * pivot * inv * inv)
        unit = rows[j : j + 1] * inv
        factor = jnp.where(sub > j, cols[j] * inv, 0.0)
        rows = jnp.where(sub == j, unit, rows - factor * unit)
        for i in range(j + 1, BLOCK):
            cols[i] = cols[i] - factor * (cols[i][j : j + 1] * inv)
    done = jnp.where(lane >= base + sub, rows, 0.0)
    ut[pl.ds(base, BLOCK), :] = done
    a[...] -= outer(done, done)


def inverse_block(k, n, t, lower, upper):
    base = pl.multiple_of(BLOCK * k, BLOCK)
    sub = lax.broadcasted_iota(jnp.int32, (BLOCK, 128), 0)
    rows, turned = n[pl.ds(base, BLOCK), :], t[pl.ds(base, BLOCK), :]
    rc, tc = spread_columns(rows[:, :128], base), spread_columns(turned[:, :128], base)
    scale = jnp.zeros((BLOCK, 128), F32)
    for j in range(BLOCK):
        inv = 1.0 / rc[j][j : j + 1]
        scale = jnp.where(sub == j, inv, scale)
        down = jnp.where(sub > j, rc[j] * inv, 0.0)
        across = jnp.where(sub > j, tc[j] * inv, 0.0)
        rows = rows - jnp.concatenate([down, down], 1) * rows[j : j + 1]
        turned = turned - jnp.concatenate([across, across], 1) * turned[j : j + 1]
        for i in range(j + 1, BLOCK):
            rc[i] = rc[i] - down * rc[i][j : j + 1]
            tc[i] = tc[i] - across * tc[i][j : j + 1]
    turned = turned * jnp.concatenate([scale, scale], 1)
    lower[pl.ds(base, BLOCK), :] = rows[:, 128:]
    upper[pl.ds(base, BLOCK), :] = turned[:, 128:]
    n[...] -= outer(turned[:, :128], rows)
    t[...] -= outer(rows[:, :128], turned)


def step_kernel(psi, hpsi_far, counts, stored_far, out, hpsi, stored, bands, part, theirs, wa, wb, ra1, rb1, a1, b1, ra2,
                rb2, ab2, r3, own, srow, scol, mh, slr, slc, gram, cross, gx, gfull, s1, tops, m1c, m1r,
                raw, rawt, xt, xo, xsum, tpart, xin, xown, xr, xc, work, ut, n, t, lower, upper, zr, zc, tx, tfull,
                load, ss, rs, ss_b, rs_b, ss_p, rs_p, ss_r, rs_r, ss_c, rs_c, ss_g, rs_g, ss_h, rs_h,
                ss_s, rs_s, ss_m, rs_m, ss_k, rs_k, ss_x, rs_x, ss_y, rs_y, ss_z, rs_z,
                ss_w, rs_w, ss_v, rs_v):
    p, q, zh, y, x, zl, c = position()
    z = zh * 4 + zl
    first = c == 0
    f = jnp.where(first, y, z)
    s = jnp.where(first, z, y)
    half, slot = q // 16, q % 16
    piece_at = q // 2
    row_slot = 16 * (q % 2) + q // 2
    home = p + 16 * (q % 2)
    at_home = home == q

    def at(xx, ff, sf):
        yy, zz = jnp.where(first, ff, sf), jnp.where(first, sf, ff)
        return device(zz // 4, yy, xx, zz % 4, c)

    def loop(start, stop, body):
        def step(i, carry):
            body(i)
            return carry
        lax.fori_loop(start, stop, step, 0)

    def fetch(g):
        xx = (x + 1 + g) % 4
        return pltpu.make_async_copy(
            psi.at[:, pl.ds(pl.multiple_of(2048 * xx, 2048), 2048)], bands.at[xx], load.at[g]
        )

    fetch_panel = pltpu.make_async_copy(hpsi_far, hpsi, load.at[4])
    fetch_matrix = pltpu.make_async_copy(stored_far, stored, load.at[5])
    fetch_panel.start()
    for g in range(4):
        fetch(g).start()
    fetch_matrix.start()

    partner = device(zh, y, x, zl, 1 - c)
    barrier = pltpu.get_barrier_semaphore()

    def hail(who):
        pl.semaphore_signal(barrier, inc=1, device_id=who, device_id_type=MESH)

    def hail_unless_me(who):
        @pl.when((who[0] != p) | (who[1] != q))
        def _():
            hail(who)

    hail(partner)
    for d in range(1, 4):
        hail(at((x + d) % 4, f, s))
    for d in range(1, 8):
        hail(at(x, (f + d) % 8, s))
        hail(at(x, f, (s + d) % 8))
    loop(1, 16, lambda d: hail(((p + d) % 16, q)))
    loop(1, 32, lambda d: hail((p, (q + d) % 32)))
    loop(0, 16, lambda j: hail_unless_me((slot, 2 * j + half)))

    fetch_panel.wait()
    live = lax.broadcasted_iota(jnp.int32, (256, 128), 0) < counts[0]
    panel = jnp.where(live, hpsi[...].astype(F32), 0.0).astype(BF16)
    def multiply(g):
        xx = (x + 1 + g) % 4
        fetch(g).wait()

        def four(i):
            for u in range(4):
                at_chunk = pl.ds(pl.multiple_of(512 * i + 128 * u, 128), 128)
                part[xx, i, u // 2, u % 2] = dot(bands[xx, :, at_chunk], panel, 0, 0).reshape(8, 16, 128)

        loop(0, 4, four)

    def swap(g):
        xx = (x + 1 + g) % 4
        return send(part.at[xx, :, 1 - c], theirs.at[xx], ss_p.at[g], rs_p.at[g], partner)

    for g in range(4):
        multiply(g)
    fetch_matrix.wait()

    def halves_of(i):
        return [pl.ds(32 * i + k, 16, stride=2) for k in range(2)]

    for h in range(2):
        for j in range(16):
            for k, lines in enumerate(halves_of(2 * j + h)):
                mh[16 * h + j, :, 128 * k : 128 * k + 128] = stored[lines, :]

    raw[...] = mh[0]
    in_rim = (q >= 8) & (q < 16)
    rim = jnp.clip(q - 8, 0, 7) // 2

    @pl.when(in_rim)
    def _():
        for h in range(2):
            rawt[h] = mh[16 * h : 16 * h + 16, :, :128].reshape(256, 128).T[:16]
        m1r[:, rim, c] = rawt[...]


    pl.semaphore_wait(barrier, 18 + 15 + 31 + 15 + jnp.where(at_home, 0, 1))
    for g in range(4):
        swap(g).start()

    from_panel = jnp.maximum(p - 8, 0)

    def put_m(d):
        return send(raw, m1c.at[from_panel], ss_m.at[d], rs_m.at[from_panel], ((p + d) % 16, q))

    def put_k(d):
        return send(rawt, m1r.at[:, rim, c], ss_k.at[d], rs_k.at[rim], (p, (q + 2 * d) % 32))

    @pl.when(in_rim)
    def _():
        loop(1, 16, lambda d: put_k(d).start())

    def stage_a(g):
        xx = (x + 1 + g) % 4
        return send(wa.at[xx], ra1.at[g], ss.at[g], rs.at[g], at(xx, f, s))

    def stage_b(g, d):
        xx, ff = (x + 1 + g) % 4, (f + d) % 8
        return send(
            wb.at[ff, xx], rb1.at[d - 1, xx], ss_b.at[8 * g + d], rs_b.at[8 * g + d], at(x, ff, s)
        )

    for g in range(4):
        xx = (x + 1 + g) % 4
        swap(g).wait()

        def join(ff):
            for sf in range(8):
                yy, zz = jnp.where(first, ff, sf), jnp.where(first, sf, ff)
                hh, ll = zz // 4, zz % 4
                total = part[xx, ll, c, hh, yy] + theirs[xx, ll, hh, yy]
                wa[xx, ff, sf] = total[:8]
                wb[ff, xx, sf] = total[8:]

        loop(0, 8, join)
        if g < 3:
            stage_a(g).start()
        loop(1, 8, lambda d: stage_b(g, d).start())

    for g in range(4):
        loop(1, 8, lambda d: stage_b(g, d).wait())

    def sum_b1(i):
        total = wb[f, i]
        for d in range(7):
            total += rb1[d, i]
        b1[i] = total

    loop(0, 4, sum_b1)
    copies_b = []
    for d in range(1, 4):
        xx = (x + d) % 4
        copies_b.append(send(b1.at[xx], rb2.at[d - 1], ss.at[10 + d], rs.at[10 + d], at(xx, f, s)))
        copies_b[-1].start()
    for g in range(3):
        stage_a(g).wait()

    def sum_a1(i):
        total = wa[x, i]
        for d in range(3):
            total += ra1[d, i]
        a1[i] = total

    loop(0, 8, sum_a1)
    copies_a = []
    for d in range(1, 8):
        ff = (f + d) % 8
        copies_a.append(send(a1.at[ff], ra2.at[d - 1], ss.at[13 + d], rs.at[13 + d], at(x, ff, s)))
        copies_a[-1].start()

    @pl.when(p >= 8)
    def _():
        m1c[from_panel] = raw[...]
        loop(1, 16, lambda d: put_m(d).start())

    for copy in copies_b:
        copy.wait()
    ab2[:, 1] = b1[x] + rb2[0] + rb2[1] + rb2[2]
    for copy in copies_a:
        copy.wait()
    total = a1[f]
    for d in range(7):
        total += ra2[d]
    ab2[:, 0] = total
    copies = []
    for d in range(1, 8):
        sf = (s + d) % 8
        copies.append(send(ab2.at[sf], r3.at[d - 1], ss.at[20 + d], rs.at[20 + d], at(x, f, sf)))
        copies[-1].start()
    for copy in copies:
        copy.wait()
    total = ab2[s]
    for d in range(7):
        total += r3[d]
    own[...] = total.reshape(16, 128)
    srow[row_slot] = own[...]

    def to_row_group(src, dst, sem, landed):
        return lambda d: send(src, dst, sem.at[d], landed, ((p + d) % 16, q))

    def to_col_group(src, dst, sem, landed):
        return lambda d: send(src, dst, sem.at[d], landed, (p, (q + d) % 32))

    def start_all(copy, stop):
        loop(1, stop, lambda d: copy(d).start())

    def sent_all(copy, stop):
        loop(1, stop, lambda d: copy(d).wait_send())

    def landed(dst, sem):
        send(dst, dst, ss.at[0], sem, (p, q)).wait_recv()

    put_r = to_col_group(own, srow.at[row_slot], ss_r, rs_r.at[row_slot])

    def put_c(d):
        return send(own, scol.at[q // 2], ss_c.at[d], rs_c.at[q // 2], ((p + d) % 16, home))

    start_all(put_r, 32)
    start_all(put_c, 16)

    @pl.when(at_home)
    def _():
        scol[q // 2] = own[...]

    @pl.when(jnp.logical_not(at_home))
    def _():
        put_c(0).start()

    relay = send(m1r.at[:, :, c], m1r.at[:, :, c], ss.at[28], rs.at[28], partner)

    def take_rim(i):
        @pl.when(8 + 2 * i + c != q)
        def _():
            landed(m1r.at[:, i, c], rs_k.at[i])

    loop(0, 4, take_rim)
    relay.start()

    def take_mc(i):
        @pl.when(i + 8 != p)
        def _():
            landed(m1c.at[i], rs_m.at[i])

    def take_col(buffer, sem):
        def take(j):
            @pl.when((slot != p) | (2 * j + half != q))
            def _():
                landed(buffer.at[j], sem.at[j])

        loop(0, 16, take)

    def take_row(buffer, sem):
        def take(d):
            owner = (q + d) % 32
            at_slot = 16 * (owner % 2) + owner // 2
            landed(buffer.at[at_slot], sem.at[at_slot])

        loop(1, 32, take)

    take_row(srow, rs_r)
    zero = jnp.zeros((16, 128), F32)
    slr[...] = srow[...]

    @pl.when(p < 8)
    def _():
        slr[0] = zero

    low = slr[...].reshape(512, 128)
    gram[...] = dot(low, low, 0, 0, HIGH)
    at_piece = pl.ds(pl.multiple_of(8 * piece_at, 8), 8)
    gx[p] = gram[at_piece, :]
    put_g = to_row_group(gx.at[p], gx.at[p], ss_g, rs_g.at[p])
    start_all(put_g, 16)
    put_s = to_row_group(s1.at[from_panel], s1.at[from_panel], ss_s, rs_s.at[from_panel])

    lane = lax.broadcasted_iota(jnp.int32, (16, 128), 1)
    in_left = (lane < 16) & (q < 8)

    @pl.when(q < 8)
    def _():
        left = pltpu.roll(srow[...].reshape(512, 128), (128 - 16 * (q % 8)) % 128, 1).reshape(32, 16, 128)
        mh[:, :, :128] = jnp.where(in_left[None], left, mh[:, :, :128])

    take_col(scol, rs_c)
    slc[...] = scol[...]

    @pl.when(q < 8)
    def _():
        slc[0] = zero

    @pl.when(p < 8)
    def _():
        turned = pltpu.roll(scol[...].reshape(256, 128), (128 - 16 * (p % 8)) % 128, 1)
        upper_rows = turned.T[:16]
        mh[0, :, :128] = jnp.where(
            in_left, 0.5 * (mh[0, :, :128] + upper_rows[:, :128]), upper_rows[:, :128]
        )
        mh[0, :, 128:] = upper_rows[:, 128:]

    xpart = dot3(mh[...].reshape(512, 256), slc[...].reshape(256, 128), 1, 0)
    xt[:, :, :16] = xpart.reshape(2, 16, 16, 128)
    tpart[...] = dot3(low, xpart, 0, 0)
    for h in range(2):
        xt[h, :, 16:] = tpart[...].reshape(16, 8, 128)
    pair = send(xt.at[1 - c], xo, ss.at[29], rs.at[29], partner)
    pair.start()
    pair.wait()
    xsum[...] = xt[c] + xo[...]

    def put_x(d):
        to = (piece_at + d) % 16
        return send(xsum.at[to], xin.at[piece_at], ss_x.at[d], rs_x.at[piece_at], (p, 2 * to + c))

    start_all(put_x, 16)
    relay.wait_recv()
    cross[...] = dot3(m1r[0].reshape(128, 256), low[:256], 1, 0) + dot3(
        m1r[1].reshape(128, 256), low[256:], 1, 0
    )
    @pl.when(p >= 8)
    def _():
        s1[from_panel, 0] = srow[0]
        s1[from_panel, 1] = m1r[0].reshape(128, 256)[:, :128].T[:16]
        start_all(put_s, 16)

    loop(0, 8, take_mc)
    sent_all(put_r, 32)
    sent_all(put_c, 16)

    @pl.when(jnp.logical_not(at_home))
    def _():
        put_c(0).wait_send()

    @pl.when(p >= 8)
    def _():
        sent_all(put_m, 16)

    @pl.when(in_rim)
    def _():
        sent_all(put_k, 16)

    def all_landed(buffer, sem, count, me):
        loop(1, count, lambda d: landed(buffer.at[(me + d) % count], sem.at[(me + d) % count]))

    def total_of(buffer, count):
        total = buffer[0]
        for i in range(1, count):
            total += buffer[i]
        return total

    def put_piece(full, sem, got):
        def copy(d):
            to = (piece_at + d) % 16
            return send(full.at[piece_at], full.at[piece_at], sem.at[d], got.at[piece_at], (p, 2 * to + c))
        return copy

    all_landed(gx, rs_g, 16, p)
    gfull[piece_at] = total_of(gx, 16)
    put_h = put_piece(gfull, ss_h, rs_h)
    start_all(put_h, 16)

    all_landed(xin, rs_x, 16, piece_at)
    xin[piece_at] = xsum[piece_at]
    both = total_of(xin, 16)
    xown[...] = both[:16]
    tx[p, 0] = both[16:]
    tx[p, 1] = cross[at_piece, :]
    xr[row_slot] = both[:16]
    put_w = to_row_group(tx.at[p], tx.at[p], ss_w, rs_w.at[p])
    start_all(put_w, 16)
    put_y = to_col_group(xown, xr.at[row_slot], ss_y, rs_y.at[row_slot])
    start_all(put_y, 32)

    def put_z(d):
        return send(xown, xc.at[q // 2], ss_z.at[d], rs_z.at[q // 2], ((p + d) % 16, home))

    start_all(put_z, 16)

    @pl.when(at_home)
    def _():
        xc[q // 2] = xown[...]

    @pl.when(jnp.logical_not(at_home))
    def _():
        put_z(0).start()

    sent_all(put_g, 16)
    sent_all(put_x, 16)

    @pl.when(p >= 8)
    def _():
        sent_all(put_s, 16)

    all_landed(gfull, rs_h, 16, piece_at)
    gram_all = gfull[...].reshape(128, 128)
    work[...] = gram_all
    loop(0, 128 // BLOCK, lambda k: cholesky_block(k, work, ut))

    def take_from_panel(i):
        @pl.when(i + 8 != p)
        def _():
            landed(s1.at[i], rs_s.at[i])

    loop(0, 8, take_from_panel)
    tops[...] = s1[:, 0].reshape(128, 128)
    normal = gram_all - dot(ut[...], tops[...], 0, 0, HIGH)
    eye = (
        lax.broadcasted_iota(jnp.int32, (128, 128), 0) == lax.broadcasted_iota(jnp.int32, (128, 128), 1)
    ).astype(F32)
    n[:, :128] = normal
    n[:, 128:] = eye
    t[:, :128] = normal.T
    t[:, 128:] = eye
    loop(0, 3, lambda k: inverse_block(k, n, t, lower, upper))
    all_landed(tx, rs_w, 16, p)
    tfull[piece_at] = total_of(tx, 16)
    put_v = put_piece(tfull, ss_v, rs_v)
    start_all(put_v, 16)
    loop(3, 128 // BLOCK, lambda k: inverse_block(k, n, t, lower, upper))
    inverse_t = dot(lower[...], upper[...], 0, 0, HIGH)
    work[...] = inverse_t
    root = ut[...]
    rest = dot(dot(root, s1[:, 1].reshape(128, 128), 0, 0, HIGH), root, 1, 0, HIGH)

    @pl.when(p >= 8)
    def _():
        slr[0] -= ut[pl.ds(pl.multiple_of(16 * from_panel, 16), 16), :]

    @pl.when((q >= 8) & (q < 16))
    def _():
        slc[0] -= ut[pl.ds(pl.multiple_of(16 * jnp.clip(q - 8, 0, 7), 16), 16), :]

    all_lanes = lax.broadcasted_iota(jnp.int32, (128, 128), 1)

    def patched(block, at_tile):
        fresh = pltpu.roll(tops[...], (128 - 16 * (at_tile % 8)) % 128, 1)
        return jnp.where((all_lanes < 16) & (at_tile < 8), fresh, block)

    rim0 = m1r[0].reshape(128, 256)
    rim0 = jnp.concatenate([patched(rim0[:, :128], p), rim0[:, 128:]], 1)
    rimc = m1c[...].reshape(128, 256)
    rimc = jnp.concatenate([patched(rimc[:, :128], q), rimc[:, 128:]], 1)
    zr[...] = jnp.concatenate(
        [dot3(rim0, root, 0, 0), dot3(m1r[1].reshape(128, 256), root, 0, 0)], 0
    )
    zc[...] = dot3(rimc, root, 0, 0)
    take_row(xr, rs_y)
    take_col(xc, rs_z)
    acols = dot3(xc[...].reshape(256, 128) - zc[...], work[...], 1, 0)
    ycols = slc[...].reshape(256, 128)
    rh, rl = halves(jnp.concatenate([acols, ycols], 1))
    for h in range(4):
        rows = slr[pl.ds(8 * h, 8)].reshape(128, 128)
        brows = dot3(
            xr[pl.ds(8 * h, 8)].reshape(128, 128) - zr[pl.ds(128 * h, 128), :], work[...], 1, 0
        )
        lh, ll = halves(jnp.concatenate([rows, brows], 1))
        change = dot(lh, rh, 1, 1) + (dot(lh, rl, 1, 1) + dot(ll, rh, 1, 1))
        mh[pl.ds(8 * h, 8)] = mh[pl.ds(8 * h, 8)] - change.reshape(8, 16, 256)
    sent_all(put_h, 16)
    sent_all(put_y, 32)
    sent_all(put_z, 16)
    sent_all(put_w, 16)

    @pl.when(jnp.logical_not(at_home))
    def _():
        put_z(0).wait_send()

    all_landed(tfull, rs_v, 16, piece_at)
    turn = dot(tfull[:, 1].reshape(128, 128), root, 0, 0, HIGH)
    wmat = tfull[:, 0].reshape(128, 128) + (rest - (turn + turn.T))
    core = dot(dot(work[...], wmat, 0, 0, HIGH), work[...], 1, 0, HIGH)
    ch, cl = halves(dot3(ycols, core, 1, 1))
    for h in range(4):
        lh, ll = halves(slr[pl.ds(8 * h, 8)].reshape(128, 128))
        change = dot(lh, ch, 1, 1) + (dot(lh, cl, 1, 1) + dot(ll, ch, 1, 1))
        for i in range(8):
            at_tile = 8 * h + i
            tile = mh[at_tile] + change[16 * i : 16 * i + 16]
            for k, lines in enumerate(halves_of(2 * (at_tile % 16) + at_tile // 16)):
                out[lines, :] = tile[:, 128 * k : 128 * k + 128]

    sent_all(put_v, 16)
    relay.wait_send()


def step(psi, hpsi, counts, stored):
    vmem = pl.BlockSpec(memory_space=pltpu.VMEM)
    far = pl.BlockSpec(memory_space=pltpu.HBM)

    def room(*dims):
        return pltpu.VMEM(dims, F32)

    sems = [6, 32, 32, 32, 32, 4, 4, 32, 32, 16, 16, 16, 16, 16, 16, 16, 8, 16, 8, 16, 16, 32, 32, 32, 32, 16, 16, 16, 16, 16, 16]
    return pl.pallas_call(
        step_kernel,
        name="step",
        out_shape=jax.ShapeDtypeStruct((1024, 128), F32),
        in_specs=[far, far, pl.BlockSpec(memory_space=pltpu.SMEM), far],
        out_specs=vmem,
        scratch_shapes=[
            pltpu.VMEM((256, 128), BF16), room(1024, 128), pltpu.VMEM((4, 256, 2048), BF16), room(4, 4, 2, 2, 8, 16, 128),
            room(4, 4, 2, 8, 16, 128), room(4, 8, 8, 8, 128), room(8, 4, 8, 8, 128),
            room(3, 8, 8, 8, 128), room(7, 4, 8, 8, 128), room(8, 8, 8, 128), room(4, 8, 8, 128),
            room(7, 8, 8, 128), room(3, 8, 8, 128), room(8, 2, 8, 128), room(7, 2, 8, 128),
            room(16, 128),
            room(32, 16, 128), room(16, 16, 128), room(32, 16, 256), room(32, 16, 128),
            room(16, 16, 128), room(128, 128), room(128, 128), room(16, 8, 128),
            room(16, 8, 128), room(8, 2, 16, 128), room(128, 128), room(8, 16, 256),
            room(2, 4, 2, 16, 256), room(16, 256), room(2, 16, 256), room(2, 16, 24, 128), room(16, 24, 128), room(16, 24, 128), room(128, 128),
            room(16, 24, 128), room(16, 128), room(32, 16, 128), room(16, 16, 128),
            room(128, 128), room(128, 128), room(128, 256), room(128, 256), room(128, 128),
            room(128, 128), room(512, 128), room(256, 128), room(16, 2, 8, 128), room(16, 2, 8, 128),
        ] + [pltpu.SemaphoreType.DMA((k,)) for k in sems],
        compiler_params=pltpu.CompilerParams(
            collective_id=1, has_side_effects=True, vmem_limit_bytes=48 << 20
        ),
    )(psi, hpsi, counts, stored)


def per_device(psi, hpsi, slab_counts, matrix):
    def stay(array):
        return pltpu.with_memory_space_constraint(array, pltpu.HBM)

    return step(
        stay(psi), stay(hpsi), slab_counts, stay(matrix.reshape(1024, 128))
    ).reshape(matrix.shape)


def solution(mesh):
    in_specs = (
        P(("row", "col"), None),
        P(("row", "col"), None),
        P(("row", "col")),
        P("row", None, "col", None),
    )
    out_specs = P("row", None, "col", None)
    return jax.shard_map(
        per_device, mesh=mesh, in_specs=in_specs, out_specs=out_specs, check_vma=False
    )
```

```python
import jax
import jax.numpy as jnp
from jax import lax
from jax.sharding import PartitionSpec as P
from jax.experimental import pallas as pl
from jax.experimental.pallas import tpu as pltpu

MESH = pl.DeviceIdType.MESH
HIGH = lax.Precision.HIGHEST
BLOCK = 16
F32, BF16 = jnp.float32, jnp.bfloat16


def position():
    p, q = lax.axis_index("row"), lax.axis_index("col")
    return p, q, p // 8, p % 8, q // 8, (q // 2) % 4, q % 2


def device(zh, y, x, zl, c):
    return (zh * 8 + y, x * 8 + zl * 2 + c)


def send(src, dst, send_sem, recv_sem, target):
    return pltpu.make_async_remote_copy(
        src_ref=src, dst_ref=dst, send_sem=send_sem, recv_sem=recv_sem,
        device_id=target, device_id_type=MESH,
    )


def dot(a, b, ca, cb, precision=None):
    return lax.dot_general(
        a, b, (((ca,), (cb,)), ((), ())), precision=precision, preferred_element_type=F32
    )


def halves(a):
    high = a.astype(BF16)
    return high, (a - high.astype(F32)).astype(BF16)


def dot3(a, b, ca, cb):
    (ah, al), (bh, bl) = halves(a), halves(b)
    return dot(ah, bh, ca, cb) + (dot(ah, bl, ca, cb) + dot(al, bh, ca, cb))


def thirds(a):
    high = a.astype(BF16).astype(F32)
    rest = a - high
    middle = rest.astype(BF16).astype(F32)
    return high, middle, rest - middle


def outer(a, b):
    (ah, am, al), (bh, bm, bl) = thirds(a), thirds(b)
    left = jnp.concatenate([ah, ah, am, am, ah, al], 0).astype(BF16)
    right = jnp.concatenate([bh, bm, bh, bm, bl, bh], 0).astype(BF16)
    return dot(left, right, 0, 0)


def spread_columns(rows, base):
    turned = pltpu.roll(rows, (128 - base) % 128, 1)
    return [jnp.broadcast_to(turned[:, j : j + 1], (BLOCK, 128)) for j in range(BLOCK)]


def cholesky_block(k, a, ut):
    base = pl.multiple_of(BLOCK * k, BLOCK)
    sub = lax.broadcasted_iota(jnp.int32, (BLOCK, 128), 0)
    lane = lax.broadcasted_iota(jnp.int32, (BLOCK, 128), 1)
    rows = a[pl.ds(base, BLOCK), :]
    cols = spread_columns(rows, base)
    for j in range(BLOCK):
        pivot = cols[j][j : j + 1]
        inv = lax.rsqrt(pivot)
        inv = inv * (1.5 - 0.5 * pivot * inv * inv)
        unit = rows[j : j + 1] * inv
        factor = jnp.where(sub > j, cols[j] * inv, 0.0)
        rows = jnp.where(sub == j, unit, rows - factor * unit)
        for i in range(j + 1, BLOCK):
            cols[i] = cols[i] - factor * (cols[i][j : j + 1] * inv)
    done = jnp.where(lane >= base + sub, rows, 0.0)
    ut[pl.ds(base, BLOCK), :] = done
    a[...] -= outer(done, done)


def inverse_block(k, n, t, lower, upper):
    base = pl.multiple_of(BLOCK * k, BLOCK)
    sub = lax.broadcasted_iota(jnp.int32, (BLOCK, 128), 0)
    rows, turned = n[pl.ds(base, BLOCK), :], t[pl.ds(base, BLOCK), :]
    rc, tc = spread_columns(rows[:, :128], base), spread_columns(turned[:, :128], base)
    scale = jnp.zeros((BLOCK, 128), F32)
    for j in range(BLOCK):
        inv = 1.0 / rc[j][j : j + 1]
        scale = jnp.where(sub == j, inv, scale)
        down = jnp.where(sub > j, rc[j] * inv, 0.0)
        across = jnp.where(sub > j, tc[j] * inv, 0.0)
        rows = rows - jnp.concatenate([down, down], 1) * rows[j : j + 1]
        turned = turned - jnp.concatenate([across, across], 1) * turned[j : j + 1]
        for i in range(j + 1, BLOCK):
            rc[i] = rc[i] - down * rc[i][j : j + 1]
            tc[i] = tc[i] - across * tc[i][j : j + 1]
    turned = turned * jnp.concatenate([scale, scale], 1)
    lower[pl.ds(base, BLOCK), :] = rows[:, 128:]
    upper[pl.ds(base, BLOCK), :] = turned[:, 128:]
    n[...] -= outer(turned[:, :128], rows)
    t[...] -= outer(rows[:, :128], turned)


def step_kernel(psi, hpsi_far, counts, stored_far, out, hpsi, stored, bands, part, theirs, wa, wb, ra1, rb1, a1, b1, ra2,
                rb2, ab2, r3, own, srow, scol, mh, slr, slc, gram, cross, gx, gfull, s1, tops, m1c, m1r,
                raw, rawt, xt, xo, xsum, tpart, xin, xown, xr, xc, work, ut, n, t, lower, upper, zr, zc, tx, tfull,
                load, ss, rs, ss_b, rs_b, ss_p, rs_p, ss_r, rs_r, ss_c, rs_c, ss_g, rs_g, ss_h, rs_h,
                ss_s, rs_s, ss_m, rs_m, ss_k, rs_k, ss_x, rs_x, ss_y, rs_y, ss_z, rs_z,
                ss_w, rs_w, ss_v, rs_v, ss_e, rs_e):
    p, q, zh, y, x, zl, c = position()
    z = zh * 4 + zl
    first = c == 0
    f = jnp.where(first, y, z)
    s = jnp.where(first, z, y)
    half, slot = q // 16, q % 16
    piece_at = q // 2
    row_slot = 16 * (q % 2) + q // 2
    home = p + 16 * (q % 2)
    at_home = home == q

    def at(xx, ff, sf):
        yy, zz = jnp.where(first, ff, sf), jnp.where(first, sf, ff)
        return device(zz // 4, yy, xx, zz % 4, c)

    def loop(start, stop, body):
        def step(i, carry):
            body(i)
            return carry
        lax.fori_loop(start, stop, step, 0)

    def fetch(g):
        xx = (x + 1 + g) % 4
        return pltpu.make_async_copy(
            psi.at[:, pl.ds(pl.multiple_of(2048 * xx, 2048), 2048)], bands.at[xx], load.at[g]
        )

    fetch_panel = pltpu.make_async_copy(hpsi_far, hpsi, load.at[4])
    fetch_matrix = pltpu.make_async_copy(stored_far, stored, load.at[5])
    fetch_panel.start()
    for g in range(4):
        fetch(g).start()
    fetch_matrix.start()

    partner = device(zh, y, x, zl, 1 - c)
    barrier = pltpu.get_barrier_semaphore()

    def hail(who):
        pl.semaphore_signal(barrier, inc=1, device_id=who, device_id_type=MESH)

    def hail_unless_me(who):
        @pl.when((who[0] != p) | (who[1] != q))
        def _():
            hail(who)

    hail(partner)
    for d in range(1, 4):
        hail(at((x + d) % 4, f, s))
    for d in range(1, 8):
        hail(at(x, (f + d) % 8, s))
        hail(at(x, f, (s + d) % 8))
    loop(1, 16, lambda d: hail(((p + d) % 16, q)))
    loop(1, 32, lambda d: hail((p, (q + d) % 32)))
    loop(0, 16, lambda j: hail_unless_me((slot, 2 * j + half)))

    fetch_panel.wait()
    live = lax.broadcasted_iota(jnp.int32, (256, 128), 0) < counts[0]
    panel = jnp.where(live, hpsi[...].astype(F32), 0.0).astype(BF16)
    def multiply(g):
        xx = (x + 1 + g) % 4
        fetch(g).wait()

        def four(i):
            for u in range(4):
                at_chunk = pl.ds(pl.multiple_of(512 * i + 128 * u, 128), 128)
                part[xx, i, u // 2, u % 2] = dot(bands[xx, :, at_chunk], panel, 0, 0).reshape(8, 16, 128)

        loop(0, 4, four)

    def swap(g):
        xx = (x + 1 + g) % 4
        return send(part.at[xx, :, 1 - c], theirs.at[xx], ss_p.at[g], rs_p.at[g], partner)

    for g in range(4):
        multiply(g)
    fetch_matrix.wait()

    def halves_of(i):
        return [pl.ds(32 * i + k, 16, stride=2) for k in range(2)]

    for h in range(2):
        for j in range(16):
            for k, lines in enumerate(halves_of(2 * j + h)):
                mh[16 * h + j, :, 128 * k : 128 * k + 128] = stored[lines, :]

    raw[...] = mh[0]
    in_rim = (q >= 8) & (q < 16)
    rim = jnp.clip(q - 8, 0, 7) // 2

    @pl.when(in_rim)
    def _():
        for h in range(2):
            rawt[h] = mh[16 * h : 16 * h + 16, :, :128].reshape(256, 128).T[:16]
        m1r[:, rim, c] = rawt[...]


    pl.semaphore_wait(barrier, 18 + 15 + 31 + 15 + jnp.where(at_home, 0, 1))
    for g in range(4):
        swap(g).start()

    from_panel = jnp.maximum(p - 8, 0)

    def put_m(d):
        return send(raw, m1c.at[from_panel], ss_m.at[d], rs_m.at[from_panel], ((p + d) % 16, q))

    def put_k(d):
        return send(rawt, m1r.at[:, rim, c], ss_k.at[d], rs_k.at[rim], (p, (q + 2 * d) % 32))

    @pl.when(in_rim)
    def _():
        loop(1, 16, lambda d: put_k(d).start())

    def stage_a(g):
        xx = (x + 1 + g) % 4
        return send(wa.at[xx], ra1.at[g], ss.at[g], rs.at[g], at(xx, f, s))

    def stage_b(g, d):
        xx, ff = (x + 1 + g) % 4, (f + d) % 8
        return send(
            wb.at[ff, xx], rb1.at[d - 1, xx], ss_b.at[8 * g + d], rs_b.at[8 * g + d], at(x, ff, s)
        )

    for g in range(4):
        xx = (x + 1 + g) % 4
        swap(g).wait()

        def join(ff):
            for sf in range(8):
                yy, zz = jnp.where(first, ff, sf), jnp.where(first, sf, ff)
                hh, ll = zz // 4, zz % 4
                total = part[xx, ll, c, hh, yy] + theirs[xx, ll, hh, yy]
                wa[xx, ff, sf] = total[:8]
                wb[ff, xx, sf] = total[8:]

        loop(0, 8, join)
        if g < 3:
            stage_a(g).start()
        loop(1, 8, lambda d: stage_b(g, d).start())

    for g in range(4):
        loop(1, 8, lambda d: stage_b(g, d).wait())

    def sum_b1(i):
        total = wb[f, i]
        for d in range(7):
            total += rb1[d, i]
        b1[i] = total

    loop(0, 4, sum_b1)
    copies_b = []
    for d in range(1, 4):
        xx = (x + d) % 4
        copies_b.append(send(b1.at[xx], rb2.at[d - 1], ss.at[10 + d], rs.at[10 + d], at(xx, f, s)))
        copies_b[-1].start()
    for g in range(3):
        stage_a(g).wait()

    def sum_a1(i):
        total = wa[x, i]
        for d in range(3):
            total += ra1[d, i]
        a1[i] = total

    loop(0, 8, sum_a1)
    copies_a = []
    for d in range(1, 8):
        ff = (f + d) % 8
        copies_a.append(send(a1.at[ff], ra2.at[d - 1], ss.at[13 + d], rs.at[13 + d], at(x, ff, s)))
        copies_a[-1].start()

    @pl.when(p >= 8)
    def _():
        m1c[from_panel] = raw[...]
        loop(1, 16, lambda d: put_m(d).start())

    for copy in copies_b:
        copy.wait()
    ab2[:, 1] = b1[x] + rb2[0] + rb2[1] + rb2[2]
    for copy in copies_a:
        copy.wait()
    total = a1[f]
    for d in range(7):
        total += ra2[d]
    ab2[:, 0] = total
    copies = []
    for d in range(1, 8):
        sf = (s + d) % 8
        copies.append(send(ab2.at[sf], r3.at[d - 1], ss.at[20 + d], rs.at[20 + d], at(x, f, sf)))
        copies[-1].start()
    for copy in copies:
        copy.wait()
    total = ab2[s]
    for d in range(7):
        total += r3[d]
    own[...] = total.reshape(16, 128)
    srow[row_slot] = own[...]

    def to_row_group(src, dst, sem, landed):
        return lambda d: send(src, dst, sem.at[d], landed, ((p + d) % 16, q))

    def to_col_group(src, dst, sem, landed):
        return lambda d: send(src, dst, sem.at[d], landed, (p, (q + d) % 32))

    def start_all(copy, stop):
        loop(1, stop, lambda d: copy(d).start())

    def sent_all(copy, stop):
        loop(1, stop, lambda d: copy(d).wait_send())

    def landed(dst, sem):
        send(dst, dst, ss.at[0], sem, (p, q)).wait_recv()

    put_r = to_col_group(own, srow.at[row_slot], ss_r, rs_r.at[0])

    def put_c(d):
        return send(own, scol.at[q // 2], ss_c.at[d], rs_c.at[0], ((p + d) % 16, home))

    start_all(put_r, 32)
    start_all(put_c, 16)

    @pl.when(at_home)
    def _():
        scol[q // 2] = own[...]

    @pl.when(jnp.logical_not(at_home))
    def _():
        put_c(0).start()

    relay = send(m1r.at[:, :, c], m1r.at[:, :, c], ss.at[28], rs.at[28], partner)

    def take_rim(i):
        @pl.when(8 + 2 * i + c != q)
        def _():
            landed(m1r.at[:, i, c], rs_k.at[i])

    loop(0, 4, take_rim)
    relay.start()

    def take_mc(i):
        @pl.when(i + 8 != p)
        def _():
            landed(m1c.at[i], rs_m.at[i])

    def take_col(buffer, sem):
        @pl.when(at_home)
        def _():
            landed(buffer.at[pl.ds(0, 15)], sem.at[0])

        @pl.when(jnp.logical_not(at_home))
        def _():
            landed(buffer, sem.at[0])

    def take_row(buffer, sem):
        landed(buffer.at[pl.ds(0, 31)], sem.at[0])

    take_row(srow, rs_r)
    zero = jnp.zeros((16, 128), F32)
    slr[...] = srow[...]

    @pl.when(p < 8)
    def _():
        slr[0] = zero

    low = slr[...].reshape(512, 128)
    gram[...] = dot(low, low, 0, 0, HIGH)
    at_piece = pl.ds(pl.multiple_of(8 * piece_at, 8), 8)
    gx[p] = gram[at_piece, :]
    put_g = to_row_group(gx.at[p], gx.at[p], ss_g, rs_g.at[0])
    start_all(put_g, 16)
    put_s = to_row_group(s1.at[from_panel, 0], s1.at[from_panel, 0], ss_s, rs_s.at[from_panel])
    put_e = to_row_group(s1.at[from_panel, 1], s1.at[from_panel, 1], ss_e, rs_e.at[from_panel])

    lane = lax.broadcasted_iota(jnp.int32, (16, 128), 1)
    in_left = (lane < 16) & (q < 8)

    @pl.when(q < 8)
    def _():
        left = pltpu.roll(srow[...].reshape(512, 128), (128 - 16 * (q % 8)) % 128, 1).reshape(32, 16, 128)
        mh[:, :, :128] = jnp.where(in_left[None], left, mh[:, :, :128])

    take_col(scol, rs_c)
    slc[...] = scol[...]

    @pl.when(q < 8)
    def _():
        slc[0] = zero

    @pl.when(p < 8)
    def _():
        turned = pltpu.roll(scol[...].reshape(256, 128), (128 - 16 * (p % 8)) % 128, 1)
        upper_rows = turned.T[:16]
        mh[0, :, :128] = jnp.where(
            in_left, 0.5 * (mh[0, :, :128] + upper_rows[:, :128]), upper_rows[:, :128]
        )
        mh[0, :, 128:] = upper_rows[:, 128:]

    xpart = dot3(mh[...].reshape(512, 256), slc[...].reshape(256, 128), 1, 0)
    xt[:, :, :16] = xpart.reshape(2, 16, 16, 128)
    tpart[...] = dot3(low, xpart, 0, 0)
    for h in range(2):
        xt[h, :, 16:] = tpart[...].reshape(16, 8, 128)
    pair = send(xt.at[1 - c], xo, ss.at[29], rs.at[29], partner)
    pair.start()
    pair.wait()
    xsum[...] = xt[c] + xo[...]

    def put_x(d):
        to = (piece_at + d) % 16
        return send(xsum.at[to], xin.at[piece_at], ss_x.at[d], rs_x.at[0], (p, 2 * to + c))

    start_all(put_x, 16)
    relay.wait_recv()
    cross[...] = dot3(m1r[0].reshape(128, 256), low[:256], 1, 0) + dot3(
        m1r[1].reshape(128, 256), low[256:], 1, 0
    )
    @pl.when(p >= 8)
    def _():
        s1[from_panel, 0] = srow[0]
        s1[from_panel, 1] = m1r[0].reshape(128, 256)[:, :128].T[:16]
        start_all(put_s, 16)

    loop(0, 8, take_mc)
    sent_all(put_r, 32)
    sent_all(put_c, 16)

    @pl.when(jnp.logical_not(at_home))
    def _():
        put_c(0).wait_send()

    @pl.when(p >= 8)
    def _():
        sent_all(put_m, 16)

    @pl.when(in_rim)
    def _():
        sent_all(put_k, 16)

    def all_landed(buffer, sem, count):
        landed(buffer.at[pl.ds(0, count - 1)], sem.at[0])

    def total_of(buffer, count):
        total = buffer[0]
        for i in range(1, count):
            total += buffer[i]
        return total

    def put_piece(full, sem, got):
        def copy(d):
            to = (piece_at + d) % 16
            return send(full.at[piece_at], full.at[piece_at], sem.at[d], got.at[0], (p, 2 * to + c))
        return copy

    all_landed(gx, rs_g, 16)
    gfull[piece_at] = total_of(gx, 16)
    put_h = put_piece(gfull, ss_h, rs_h)
    start_all(put_h, 16)

    all_landed(xin, rs_x, 16)
    xin[piece_at] = xsum[piece_at]
    both = total_of(xin, 16)
    xown[...] = both[:16]
    tx[p, 0] = both[16:]
    tx[p, 1] = cross[at_piece, :]
    xr[row_slot] = both[:16]
    put_w = to_row_group(tx.at[p], tx.at[p], ss_w, rs_w.at[0])
    start_all(put_w, 16)
    @pl.when(p >= 8)
    def _():
        start_all(put_e, 16)

    put_y = to_col_group(xown, xr.at[row_slot], ss_y, rs_y.at[0])
    start_all(put_y, 32)

    def put_z(d):
        return send(xown, xc.at[q // 2], ss_z.at[d], rs_z.at[0], ((p + d) % 16, home))

    start_all(put_z, 16)

    @pl.when(at_home)
    def _():
        xc[q // 2] = xown[...]

    @pl.when(jnp.logical_not(at_home))
    def _():
        put_z(0).start()

    sent_all(put_g, 16)
    sent_all(put_x, 16)

    @pl.when(p >= 8)
    def _():
        sent_all(put_s, 16)

    all_landed(gfull, rs_h, 16)
    gram_all = gfull[...].reshape(128, 128)
    work[...] = gram_all
    loop(0, 128 // BLOCK, lambda k: cholesky_block(k, work, ut))

    def take_from_panel(i):
        @pl.when(i + 8 != p)
        def _():
            landed(s1.at[i, 0], rs_s.at[i])

    loop(0, 8, take_from_panel)
    tops[...] = s1[:, 0].reshape(128, 128)
    normal = gram_all - dot(ut[...], tops[...], 0, 0, HIGH)
    eye = (
        lax.broadcasted_iota(jnp.int32, (128, 128), 0) == lax.broadcasted_iota(jnp.int32, (128, 128), 1)
    ).astype(F32)
    n[:, :128] = normal
    n[:, 128:] = eye
    t[:, :128] = normal.T
    t[:, 128:] = eye
    loop(0, 3, lambda k: inverse_block(k, n, t, lower, upper))
    all_landed(tx, rs_w, 16)
    tfull[piece_at] = total_of(tx, 16)
    put_v = put_piece(tfull, ss_v, rs_v)
    start_all(put_v, 16)
    loop(3, 128 // BLOCK, lambda k: inverse_block(k, n, t, lower, upper))
    def take_corner(i):
        @pl.when(i + 8 != p)
        def _():
            landed(s1.at[i, 1], rs_e.at[i])

    loop(0, 8, take_corner)
    inverse_t = dot(lower[...], upper[...], 0, 0, HIGH)
    work[...] = inverse_t
    root = ut[...]
    rest = dot(dot(root, s1[:, 1].reshape(128, 128), 0, 0, HIGH), root, 1, 0, HIGH)

    @pl.when(p >= 8)
    def _():
        slr[0] -= ut[pl.ds(pl.multiple_of(16 * from_panel, 16), 16), :]

    @pl.when((q >= 8) & (q < 16))
    def _():
        slc[0] -= ut[pl.ds(pl.multiple_of(16 * jnp.clip(q - 8, 0, 7), 16), 16), :]

    all_lanes = lax.broadcasted_iota(jnp.int32, (128, 128), 1)

    def patched(block, at_tile):
        fresh = pltpu.roll(tops[...], (128 - 16 * (at_tile % 8)) % 128, 1)
        return jnp.where((all_lanes < 16) & (at_tile < 8), fresh, block)

    rim0 = m1r[0].reshape(128, 256)
    rim0 = jnp.concatenate([patched(rim0[:, :128], p), rim0[:, 128:]], 1)
    rimc = m1c[...].reshape(128, 256)
    rimc = jnp.concatenate([patched(rimc[:, :128], q), rimc[:, 128:]], 1)
    zr[...] = jnp.concatenate(
        [dot3(rim0, root, 0, 0), dot3(m1r[1].reshape(128, 256), root, 0, 0)], 0
    )
    zc[...] = dot3(rimc, root, 0, 0)
    take_row(xr, rs_y)
    take_col(xc, rs_z)
    acols = dot3(xc[...].reshape(256, 128) - zc[...], work[...], 1, 0)
    ycols = slc[...].reshape(256, 128)
    rh, rl = halves(jnp.concatenate([acols, ycols], 1))
    for h in range(4):
        rows = slr[pl.ds(8 * h, 8)].reshape(128, 128)
        brows = dot3(
            xr[pl.ds(8 * h, 8)].reshape(128, 128) - zr[pl.ds(128 * h, 128), :], work[...], 1, 0
        )
        lh, ll = halves(jnp.concatenate([rows, brows], 1))
        change = dot(lh, rh, 1, 1) + (dot(lh, rl, 1, 1) + dot(ll, rh, 1, 1))
        mh[pl.ds(8 * h, 8)] = mh[pl.ds(8 * h, 8)] - change.reshape(8, 16, 256)
    sent_all(put_h, 16)
    sent_all(put_y, 32)
    sent_all(put_z, 16)
    sent_all(put_w, 16)

    @pl.when(jnp.logical_not(at_home))
    def _():
        put_z(0).wait_send()

    all_landed(tfull, rs_v, 16)
    turn = dot(tfull[:, 1].reshape(128, 128), root, 0, 0, HIGH)
    wmat = tfull[:, 0].reshape(128, 128) + (rest - (turn + turn.T))
    core = dot(dot(work[...], wmat, 0, 0, HIGH), work[...], 1, 0, HIGH)
    ch, cl = halves(dot3(ycols, core, 1, 1))
    for h in range(4):
        lh, ll = halves(slr[pl.ds(8 * h, 8)].reshape(128, 128))
        change = dot(lh, ch, 1, 1) + (dot(lh, cl, 1, 1) + dot(ll, ch, 1, 1))
        for i in range(8):
            at_tile = 8 * h + i
            tile = mh[at_tile] + change[16 * i : 16 * i + 16]
            for k, lines in enumerate(halves_of(2 * (at_tile % 16) + at_tile // 16)):
                out[lines, :] = tile[:, 128 * k : 128 * k + 128]

    sent_all(put_v, 16)

    @pl.when(p >= 8)
    def _():
        sent_all(put_e, 16)

    relay.wait_send()


def step(psi, hpsi, counts, stored):
    vmem = pl.BlockSpec(memory_space=pltpu.VMEM)
    far = pl.BlockSpec(memory_space=pltpu.HBM)

    def room(*dims):
        return pltpu.VMEM(dims, F32)

    sems = [6, 32, 32, 32, 32, 4, 4, 32, 32, 16, 16, 16, 16, 16, 16, 16, 8, 16, 8, 16, 16, 32, 32, 32, 32, 16, 16, 16, 16, 16, 16, 16, 8]
    return pl.pallas_call(
        step_kernel,
        name="step",
        out_shape=jax.ShapeDtypeStruct((1024, 128), F32),
        in_specs=[far, far, pl.BlockSpec(memory_space=pltpu.SMEM), far],
        out_specs=vmem,
        scratch_shapes=[
            pltpu.VMEM((256, 128), BF16), room(1024, 128), pltpu.VMEM((4, 256, 2048), BF16), room(4, 4, 2, 2, 8, 16, 128),
            room(4, 4, 2, 8, 16, 128), room(4, 8, 8, 8, 128), room(8, 4, 8, 8, 128),
            room(3, 8, 8, 8, 128), room(7, 4, 8, 8, 128), room(8, 8, 8, 128), room(4, 8, 8, 128),
            room(7, 8, 8, 128), room(3, 8, 8, 128), room(8, 2, 8, 128), room(7, 2, 8, 128),
            room(16, 128),
            room(32, 16, 128), room(16, 16, 128), room(32, 16, 256), room(32, 16, 128),
            room(16, 16, 128), room(128, 128), room(128, 128), room(16, 8, 128),
            room(16, 8, 128), room(8, 2, 16, 128), room(128, 128), room(8, 16, 256),
            room(2, 4, 2, 16, 256), room(16, 256), room(2, 16, 256), room(2, 16, 24, 128), room(16, 24, 128), room(16, 24, 128), room(128, 128),
            room(16, 24, 128), room(16, 128), room(32, 16, 128), room(16, 16, 128),
            room(128, 128), room(128, 128), room(128, 256), room(128, 256), room(128, 128),
            room(128, 128), room(512, 128), room(256, 128), room(16, 2, 8, 128), room(16, 2, 8, 128),
        ] + [pltpu.SemaphoreType.DMA((k,)) for k in sems],
        compiler_params=pltpu.CompilerParams(
            collective_id=1, has_side_effects=True, vmem_limit_bytes=48 << 20
        ),
    )(psi, hpsi, counts, stored)


def per_device(psi, hpsi, slab_counts, matrix):
    def stay(array):
        return pltpu.with_memory_space_constraint(array, pltpu.HBM)

    return step(
        stay(psi), stay(hpsi), slab_counts, stay(matrix.reshape(1024, 128))
    ).reshape(matrix.shape)


def solution(mesh):
    in_specs = (
        P(("row", "col"), None),
        P(("row", "col"), None),
        P(("row", "col")),
        P("row", None, "col", None),
    )
    out_specs = P("row", None, "col", None)
    return jax.shard_map(
        per_device, mesh=mesh, in_specs=in_specs, out_specs=out_specs, check_vma=False
    )
```
